32 devices in a mesh: seq: 8 (over z, x), head: 4 (over y, core).
Axes of the slice: x: 2, y: 2, z: 4, core: 2. Of those that a mesh axis runs over, the one named last changes fastest.
Arguments:
- queries: bfloat16 [8192, 2048], P('seq', 'head'), may hold values from -100 to 100
- keys: bfloat16 [8192, 2048], P('seq', 'head'), may hold values from -8 to 8
- values: bfloat16 [8192, 2048], P('seq', 'head'), may hold values from -6 to 6
- rates: float32 [8192, 8], P('seq', 'head'), may hold values from 0.001 to 0.01
- head_scale: float32 [8], P('head'), may hold values from 0.3 to 3
- w_one: float32 [8, 256, 256], P('head'), may hold values from -0.375 to 0.375
- w_three: float32 [8, 256, 256], P('head'), may hold values from -0.375 to 0.375
- w_two: float32 [8, 256, 256], P('head'), may hold values from -0.375 to 0.375
Outputs:
- mixed: float32 [8192, 2048], P('seq', 'head')
- new_one: float32 [8, 256, 256], P('head')
- new_three: float32 [8, 256, 256], P('head')
- new_two: float32 [8, 256, 256], P('head')
The draws below stay inside these ranges and needn't reach their ends.
All inputs are finite; a program needn't handle non-finite values.
Results may differ from the reference program's by a relative error of at most 0.00065.
Values may be sent and summed in bfloat16 or wider, within the bound.
No kernel may reach another device: no remote copies, remote signals or barrier semaphores. Data moves between devices by JAX's collectives and lax.ppermute only.
A program may use at most 64 MiB of HBM per device.

```python
import math
import jax
import jax.numpy as jnp
from jax import lax

HEAD_SIZE = 256
WINDOW_SPAN = 512
HEADS = 8
TOKENS = 8192


def draw_pair(key):
    base = jax.random.fold_in(key, 71)
    shape = (TOKENS, HEADS * HEAD_SIZE)
    key_vals = jnp.clip(jax.random.normal(jax.random.fold_in(base, 1), shape, jnp.float32), -6.0, 6.0)
    query_vals = jnp.clip(jax.random.normal(jax.random.fold_in(base, 2), shape, jnp.float32), -6.0, 6.0)
    return (query_vals, key_vals)


def draw_queries(key, part):
    return draw_pair(key)[0].astype(jnp.bfloat16)


def draw_keys(key, part):
    return draw_pair(key)[1].astype(jnp.bfloat16)


def shard_levels(rng, shape, cuts, low, top_value):
    gain, own = 1.0, jax.random.fold_in(rng, 6)
    for dim, shards_of in cuts:
        heights = jnp.exp(jax.random.uniform(jax.random.fold_in(own, dim), (shards_of,), jnp.float32, low / len(cuts), top_value / len(cuts)))
        gain = gain * jnp.repeat(heights, shape[dim] // shards_of).reshape([-1 if axis == dim else 1 for axis in range(len(shape))])
    return gain


def bell_draw(own_key, extent, spread, reach, shards=(), kind=jnp.bfloat16):
    result = spread * jax.random.normal(own_key, extent, jnp.float32)
    if shards:
        result = result * shard_levels(own_key, extent, shards, -0.22, 0.18)
    return jnp.clip(result, -reach, reach).astype(kind)


def setup_inputs(seed: int = 0) -> dict:
    streams_of = jax.random.split(jax.random.key(seed), 9)
    return {
        "queries": draw_queries(jax.random.fold_in(streams_of[8], 71), 0),
        "keys": draw_keys(jax.random.fold_in(streams_of[8], 71), 0),
        "values": bell_draw(streams_of[2], (TOKENS, HEADS * HEAD_SIZE), 1.0, 6.0, ((0, 8), (1, 4))),
        "rates": jnp.clip(jnp.exp(math.log(0.01) - 2.30258502 * jax.random.uniform(streams_of[3], (TOKENS, HEADS), jnp.float32) ** shard_levels(streams_of[3], (TOKENS, HEADS), ((0, 8), (1, 4)), -0.2, 0.2)), 0.001, 0.01),
        "head_scale": jnp.clip(jnp.exp(math.log(3.0) - 2.3025851 * jax.random.uniform(streams_of[4], (HEADS,), jnp.float32) ** shard_levels(streams_of[4], (HEADS,), ((0, 4),), -0.2, 0.2)), 0.3, 3.0),
        "w_one": bell_draw(streams_of[5], (HEADS, HEAD_SIZE, HEAD_SIZE), HEAD_SIZE ** -0.5, 0.375, ((0, 4),), jnp.float32),
        "w_three": bell_draw(streams_of[6], (HEADS, HEAD_SIZE, HEAD_SIZE), HEAD_SIZE ** -0.5, 0.375, ((0, 4),), jnp.float32),
        "w_two": bell_draw(streams_of[7], (HEADS, HEAD_SIZE, HEAD_SIZE), HEAD_SIZE ** -0.5, 0.375, ((0, 4),), jnp.float32),
    }


HIGH = lax.Precision.HIGHEST
EPS = 1e-06

def renorm(weight, grad):
    upd = weight + grad
    old = jnp.sqrt(lax.optimization_barrier(jnp.sum(weight * weight, axis=0, keepdims=True)) + EPS)
    cur = jnp.sqrt(lax.optimization_barrier(jnp.sum(upd * upd, axis=0, keepdims=True)) + EPS)
    return upd * (old / cur)

def one_head(inputs):
    query, key_rows, value_rows, rate, w1, w3, w2 = inputs
    kf = key_rows.astype(jnp.float32)
    vf = value_rows.astype(jnp.float32)
    qf = query.astype(jnp.float32)
    h1 = jnp.dot(kf, w1, precision=HIGH)
    h3 = jnp.dot(kf, w3, precision=HIGH)
    sg = jax.nn.sigmoid(h1)
    sil = h1 * sg
    act = sil * h3
    scaled = rate[:, None] * vf
    g2 = jnp.dot(act.T, scaled, precision=HIGH)
    dact = jnp.dot(scaled, w2.T, precision=HIGH)
    d1 = dact * h3 * sg * (1.0 + h1 * (1.0 - sg))
    d3 = dact * sil
    g1 = jnp.dot(kf.T, d1, precision=HIGH)
    g3 = jnp.dot(kf.T, d3, precision=HIGH)
    n1 = renorm(w1, g1)
    n3 = renorm(w3, g3)
    n2 = renorm(w2, g2)
    p1 = jnp.dot(qf, n1, precision=HIGH)
    p3 = jnp.dot(qf, n3, precision=HIGH)
    outer = jnp.dot(p1 * jax.nn.sigmoid(p1) * p3, n2, precision=HIGH)
    return (n1, n3, n2, outer)

def reference(queries, keys, values, rates, head_scale, w_one, w_three, w_two):
    total = queries.shape[0]
    head_group = w_one.shape[0]
    span_size = w_one.shape[1]
    qh = queries.reshape(total, head_group, span_size).transpose(1, 0, 2)
    kh = keys.reshape(total, head_group, span_size).transpose(1, 0, 2)
    value_head = values.reshape(total, head_group, span_size).transpose(1, 0, 2)
    n1, n3, n2, outer = lax.map(one_head, (qh, kh, value_head, rates.T, w_one, w_three, w_two))
    zed = outer * head_scale[:, None, None]
    mean_sq = lax.optimization_barrier(jnp.sum(zed * zed, axis=(0, 2))) / (head_group * span_size)
    ynorm = zed / jnp.sqrt(mean_sq + EPS)[None, :, None]
    block_span = min(512, total)
    kpad = jnp.concatenate([jnp.zeros((head_group, WINDOW_SPAN, span_size), jnp.bfloat16), kh], axis=1)
    padded_values = jnp.concatenate([jnp.zeros((head_group, WINDOW_SPAN, span_size), jnp.bfloat16), value_head], axis=1)
    scale = span_size ** (-0.5)

    def attend(index):
        start_offset = (index * block_span).astype(jnp.int32)
        qb = lax.dynamic_slice_in_dim(qh, start_offset, block_span, 1).astype(jnp.float32)
        kb = lax.dynamic_slice_in_dim(kpad, start_offset, block_span + WINDOW_SPAN, 1).astype(jnp.float32)
        value_block = lax.dynamic_slice_in_dim(padded_values, start_offset, block_span + WINDOW_SPAN, 1).astype(jnp.float32)
        scores = jnp.einsum('hid,hjd->hij', qb, kb) * scale
        rows = jnp.arange(block_span, dtype=jnp.int32)[:, None]
        cols = jnp.arange(block_span + WINDOW_SPAN, dtype=jnp.int32)[None, :]
        allowed = (cols > rows) & (cols <= rows + WINDOW_SPAN) & (start_offset + cols - WINDOW_SPAN >= 0)
        scores = jnp.where(allowed[None], scores, -jnp.inf)
        top = lax.optimization_barrier(jnp.max(scores, axis=-1, keepdims=True))
        expo = jnp.exp(scores - top)
        weights = (expo / lax.optimization_barrier(jnp.sum(expo, axis=-1, keepdims=True))).astype(jnp.bfloat16)
        return jnp.einsum('hij,hjd->hid', weights.astype(jnp.float32), value_block)
    attn = lax.map(attend, jnp.arange(total // block_span, dtype=jnp.int32))
    attn = attn.transpose(1, 0, 2, 3).reshape(head_group, total, span_size)
    mixed = (attn + ynorm).transpose(1, 0, 2).reshape(total, head_group * span_size).astype(jnp.float32)
    return (mixed, n1, n3, n2)
```

```python
import functools

import jax
import jax.numpy as jnp
from jax import lax
from jax.experimental import pallas as pl
from jax.experimental.pallas import tpu as pltpu
from jax.sharding import PartitionSpec as P

WINDOW_SPAN = 512
EPS = 1e-06
PAD = 16
WIRE = jnp.bfloat16
REACH = 120.0
BF = jnp.bfloat16
F32 = jnp.float32


def params(mib=24):
    return pltpu.CompilerParams(vmem_limit_bytes=mib * 1024 * 1024)


def nn(a, b):
    return lax.dot_general(a, b, (((1,), (0,)), ((), ())), preferred_element_type=F32)


def nt(a, b):
    return lax.dot_general(a, b, (((1,), (1,)), ((), ())), preferred_element_type=F32)


def split(x):
    high = x.astype(BF)
    return high, (x - high.astype(F32)).astype(BF)


def encode(x, ref):
    rows, size = x.shape
    top = jnp.max(jnp.abs(x), axis=1, keepdims=True)
    scale = (jnp.maximum(top, 1e-30) * 1.008).astype(WIRE).astype(F32)
    code = jnp.exp2(jnp.abs(x) * (2.0 * REACH / scale) - REACH)
    ref[0, 0:rows] = jnp.where(x < 0, -code, code).astype(WIRE)
    column = jnp.concatenate([scale, jnp.zeros((size - rows, 1), F32)], axis=0)
    ref[0, rows : rows + PAD] = jnp.broadcast_to(column, (size, 128)).T[0:PAD].astype(WIRE)


def decode(ref):
    rows = ref.shape[1] - PAD
    scale = ref[0, rows : rows + PAD].astype(F32).T[0:rows, 0:1]
    code = ref[0, 0:rows].astype(F32)
    size = (jnp.log2(jnp.abs(code)) + REACH) * (scale * (0.5 / REACH))
    return jnp.where(code < 0, -size, size)


def grads_body(quarter, k_ref, v_ref, r_ref, w1_ref, w3_ref, w2_ref, own_ref, p1_ref, p2_ref, p3_ref, wt_ref, acc):
    size = w1_ref.shape[1]
    tokens = k_ref.shape[0]
    head = pl.program_id(0)
    w1t, w3t, w2 = w1_ref[0].T, w3_ref[0].T, w2_ref[0]
    wt_ref[0, 0:size] = w1t
    wt_ref[0, size : 2 * size] = w3t
    wt_ref[0, 2 * size : 3 * size] = w2.T
    w1h, w1l = split(w1t)
    w3h, w3l = split(w3t)
    w2h, w2l = split(w2)
    g1 = g3 = g2 = None
    block = min(256, tokens)
    for start in range(0, tokens, block):
        kb = k_ref[start : start + block]
        vb = v_ref[start : start + block]
        rate = r_ref[pl.ds(head, 1), start : start + block]
        h1 = nt(w1h, kb) + nt(w1l, kb)
        h3 = nt(w3h, kb) + nt(w3l, kb)
        da = (nt(w2h, vb) + nt(w2l, vb)) * rate
        sg = 1.0 / (1.0 + jnp.exp(-h1))
        sil = h1 * sg
        act = sil * h3 * rate
        d3 = da * sil
        d1 = da * h3 * (sg * (1.0 + h1 * (1.0 - sg)))
        ah, al = split(act)
        d1h, d1l = split(d1)
        d3h, d3l = split(d3)
        t1 = nn(d1h, kb) + nn(d1l, kb)
        t3 = nn(d3h, kb) + nn(d3l, kb)
        t2 = nn(ah, vb) + nn(al, vb)
        g1 = t1 if g1 is None else g1 + t1
        g3 = t3 if g3 is None else g3 + t3
        g2 = t2 if g2 is None else g2 + t2
    g2 = g2.T
    acc[0:size] = g1
    acc[size : 2 * size] = g3
    acc[2 * size : 3 * size] = g2
    rows = 3 * size // 4
    q = quarter[0]
    own_ref[0] = acc[pl.ds(pl.multiple_of(q * rows, 8), rows)]
    for j, ref in ((1, p1_ref), (2, p2_ref), (3, p3_ref)):
        encode(acc[pl.ds(pl.multiple_of((q ^ j) * rows, 8), rows)], ref)


def grads(quarter, keys, values, rates_t, w1, w3, w2, first, count):
    tokens = keys.shape[0]
    size = w1.shape[1]
    rows = 3 * size // 4
    wire = jax.ShapeDtypeStruct((count, rows + PAD, size), WIRE)
    wire_spec = pl.BlockSpec((1, rows + PAD, size), lambda i, q: (i, 0, 0))
    body = functools.partial(grads_body)
    w_spec = pl.BlockSpec((1, size, size), lambda i, q: (i + first, 0, 0))
    return pl.pallas_call(
        body,
        out_shape=(
            jax.ShapeDtypeStruct((count, rows, size), F32),
            wire,
            wire,
            wire,
            jax.ShapeDtypeStruct((count, 3 * size, size), F32),
        ),
        grid_spec=pltpu.PrefetchScalarGridSpec(
            num_scalar_prefetch=1,
            grid=(count,),
            in_specs=[
                pl.BlockSpec((tokens, size), lambda i, q: (0, i + first)),
                pl.BlockSpec((tokens, size), lambda i, q: (0, i + first)),
                pl.BlockSpec((count, tokens), lambda i, q: (first // count, 0)),
                w_spec,
                w_spec,
                w_spec,
            ],
            out_specs=(
                pl.BlockSpec((1, rows, size), lambda i, q: (i, 0, 0)),
                wire_spec,
                wire_spec,
                wire_spec,
                pl.BlockSpec((1, 3 * size, size), lambda i, q: (i, 0, 0)),
            ),
            scratch_shapes=[pltpu.VMEM((3 * size, size), F32)],
        ),
        compiler_params=params(),
        cost_estimate=pl.CostEstimate(flops=count * 24 * tokens * size * size, bytes_accessed=1 << 21, transcendentals=0),
        name="grads",
    )(quarter, keys, values, rates_t, w1, w3, w2)


def gather_body(own_ref, r1_ref, r2_ref, r3_ref, out_ref):
    encode(own_ref[0] + decode(r1_ref) + (decode(r2_ref) + decode(r3_ref)), out_ref)


def per_head(body, out_shapes, *args, name, scalar=None, mib=24):
    def spec(a):
        rest = a.shape[1:]
        return pl.BlockSpec((1, *rest), lambda i, *_: (i,) + (0,) * len(rest))

    count = args[0].shape[0]
    return pl.pallas_call(
        body,
        out_shape=out_shapes,
        grid_spec=pltpu.PrefetchScalarGridSpec(
            num_scalar_prefetch=0 if scalar is None else 1,
            grid=(count,),
            in_specs=[spec(a) for a in args],
            out_specs=jax.tree.map(spec, out_shapes),
        ),
        compiler_params=params(mib),
        name=name,
    )(*(() if scalar is None else (scalar,)), *args)


def cross_body(mine_ref, other_ref, out_ref):
    encode(decode(mine_ref) + decode(other_ref), out_ref)


def renorm_body(quarter, wt_ref, mine_ref, other_ref, out_ref):
    rows = out_ref.shape[1] - PAD
    w = wt_ref[0, pl.ds(pl.multiple_of(quarter[0] * rows, 8), rows)]
    upd = w + (decode(mine_ref) + decode(other_ref))
    old = jnp.sqrt(jnp.sum(w * w, axis=1, keepdims=True) + EPS)
    cur = jnp.sqrt(jnp.sum(upd * upd, axis=1, keepdims=True) + EPS)
    encode(upd * (old / cur), out_ref)


def apply_body(quarter, q_ref, s_ref, own_ref, r1_ref, r2_ref, r3_ref, z_ref, sq_ref, n_ref):
    rows = own_ref.shape[1] - PAD
    size = q_ref.shape[1]
    tokens = q_ref.shape[0]
    q = quarter[0]
    for j, ref in enumerate((own_ref, r1_ref, r2_ref, r3_ref)):
        n_ref[0, pl.ds(pl.multiple_of((q ^ j) * rows, 8), rows)] = decode(ref)
    n1h, n1l = split(n_ref[0, 0:size])
    n3h, n3l = split(n_ref[0, size : 2 * size])
    n2h, n2l = split(n_ref[0, 2 * size : 3 * size])
    scale = s_ref[pl.program_id(0)]
    block = min(256, tokens)
    for start in range(0, tokens, block):
        qb = q_ref[start : start + block]
        p1 = nt(qb, n1h) + nt(qb, n1l)
        p3 = nt(qb, n3h) + nt(qb, n3l)
        hh, hl = split(p1 * (1.0 / (1.0 + jnp.exp(-p1))) * p3)
        zed = (nt(hh, n2h) + nt(hl, n2h) + nt(hh, n2l)) * scale
        z_ref[start : start + block] = zed
        zz = zed * zed
        half = zz[:, 0:128]
        for lane in range(128, size, 128):
            half = half + zz[:, lane : lane + 128]
        sq_ref[0, :, start : start + block] = jnp.sum(half.T, axis=0, keepdims=True)


def apply(quarter, queries, scale, own, r1, r2, r3, first):
    tokens = queries.shape[0]
    count, padded, size = own.shape
    piece = pl.BlockSpec((1, padded, size), lambda i, q: (i, 0, 0))
    return pl.pallas_call(
        apply_body,
        out_shape=(
            jax.ShapeDtypeStruct((tokens, count * size), F32),
            jax.ShapeDtypeStruct((count, 1, tokens), F32),
            jax.ShapeDtypeStruct((count, 3 * size, size), F32),
        ),
        grid_spec=pltpu.PrefetchScalarGridSpec(
            num_scalar_prefetch=1,
            grid=(count,),
            in_specs=[
                pl.BlockSpec((tokens, size), lambda i, q: (0, i + first)),
                pl.BlockSpec(memory_space=pltpu.SMEM),
                piece,
                piece,
                piece,
                piece,
            ],
            out_specs=(
                pl.BlockSpec((tokens, size), lambda i, q: (0, i)),
                pl.BlockSpec((1, 1, tokens), lambda i, q: (i, 0, 0)),
                pl.BlockSpec((1, 3 * size, size), lambda i, q: (i, 0, 0)),
            ),
        ),
        compiler_params=params(),
        cost_estimate=pl.CostEstimate(flops=count * 14 * tokens * size * size, bytes_accessed=1 << 21, transcendentals=0),
        name="apply",
    )(quarter, queries, scale, own, r1, r2, r3)


def weights_body(n_ref, o1_ref, o3_ref, o2_ref):
    size = n_ref.shape[2]
    o1_ref[0] = n_ref[0, 0:size].T
    o3_ref[0] = n_ref[0, size : 2 * size].T
    o2_ref[0] = n_ref[0, 2 * size : 3 * size].T


def attend_body(first_ref, *refs, blocks, halo):
    if halo:
        q_ref, k_ref, v_ref, hk_ref, hv_ref, out_ref = refs
    else:
        q_ref, k_ref, v_ref, out_ref = refs
    size = q_ref.shape[1]
    step = 256
    span = WINDOW_SPAN // step
    scale = size ** (-0.5)
    rows = lax.broadcasted_iota(jnp.int32, (step, step), 0)
    cols = lax.broadcasted_iota(jnp.int32, (step, step), 1)
    for place, block in enumerate(blocks):
        qb = q_ref[place * step : (place + 1) * step]
        scores, vals = [], []
        for back in range(span, -1, -1):
            source = block - back
            if source < 0:
                at = (source + span) * step
                kb, vb = hk_ref[0, at : at + step], hv_ref[0, at : at + step]
            else:
                kb, vb = k_ref[source * step : (source + 1) * step], v_ref[source * step : (source + 1) * step]
            s = nt(qb, kb) * scale
            allowed = None
            if back == 0:
                allowed = cols <= rows
            if back == span:
                allowed = cols > rows
            if source < 0:
                here = first_ref[0] == 0
                allowed = here if allowed is None else allowed & here
            if allowed is not None:
                s = jnp.where(allowed, s, -jnp.inf)
            scores.append(s)
            vals.append(vb)
        top = scores[0].max(axis=-1, keepdims=True)
        for s in scores[1:]:
            top = jnp.maximum(top, s.max(axis=-1, keepdims=True))
        expo = [jnp.exp(s - top) for s in scores]
        total = expo[0].sum(axis=-1, keepdims=True)
        for x in expo[1:]:
            total = total + x.sum(axis=-1, keepdims=True)
        inverse = 1.0 / total
        out = None
        for x, vb in zip(expo, vals):
            part = nn((x * inverse).astype(BF), vb)
            out = part if out is None else out + part
        out_ref[place * step : (place + 1) * step] = out


def attend(first, queries, keys, values, halo, blocks, size):
    tokens, width = queries.shape
    step = 256
    count = len(blocks) * step
    base = blocks[0] * step // count
    whole = pl.BlockSpec((tokens, size), lambda i, f: (0, i))
    specs = [pl.BlockSpec((count, size), lambda i, f: (base, i)), whole, whole]
    args = [queries, keys, values]
    if halo is not None:
        specs += [
            pl.BlockSpec((1, WINDOW_SPAN, size), lambda i, f: (0, 0, i)),
            pl.BlockSpec((1, WINDOW_SPAN, size), lambda i, f: (1, 0, i)),
        ]
        args += [halo, halo]
    return pl.pallas_call(
        functools.partial(attend_body, blocks=blocks, halo=halo is not None),
        out_shape=jax.ShapeDtypeStruct((count, width), F32),
        grid_spec=pltpu.PrefetchScalarGridSpec(
            num_scalar_prefetch=1,
            grid=(width // size,),
            in_specs=specs,
            out_specs=pl.BlockSpec((count, size), lambda i, f: (0, i)),
        ),
        compiler_params=params(),
        cost_estimate=pl.CostEstimate(flops=4 * count * 768 * width, bytes_accessed=1 << 21, transcendentals=count * 1536),
        name="attend_halo" if halo is not None else "attend_own",
    )(first, *args)


def tails_body(k_ref, v_ref, out_ref):
    out_ref[0] = k_ref[...]
    out_ref[1] = v_ref[...]


def tails(keys, values):
    tokens, width = keys.shape
    spec = pl.BlockSpec((WINDOW_SPAN, width), lambda i: (tokens // WINDOW_SPAN - 1, 0))
    return pl.pallas_call(
        tails_body,
        out_shape=jax.ShapeDtypeStruct((2, WINDOW_SPAN, width), keys.dtype),
        grid=(1,),
        in_specs=[spec, spec],
        out_specs=pl.BlockSpec((2, WINDOW_SPAN, width), lambda i: (0, 0, 0)),
        compiler_params=params(),
        name="tails",
    )(keys, values)


def mix_body(z_ref, r_ref, a_ref, b_ref, out_ref, *, features):
    step = pl.program_id(0)
    block = z_ref.shape[0]
    total = r_ref[...]
    inverse = 1.0 / jnp.sqrt(total / features + EPS)
    column = jnp.broadcast_to(inverse, (128, block)).T[:, 0:1]
    y = z_ref[...] * column
    low = pl.num_programs(0) // 2

    @pl.when(step < low)
    def _():
        out_ref[...] = a_ref[...] + y

    @pl.when(step >= low)
    def _():
        out_ref[...] = b_ref[...] + y


def mix(z, total, low, high, features):
    tokens, width = z.shape
    block = 256
    n = tokens // block
    half = n // 2
    return pl.pallas_call(
        functools.partial(mix_body, features=features),
        out_shape=jax.ShapeDtypeStruct((tokens, width), F32),
        grid=(n,),
        in_specs=[
            pl.BlockSpec((block, width), lambda i: (i, 0)),
            pl.BlockSpec((1, block), lambda i: (0, i)),
            pl.BlockSpec((block, width), lambda i: (jnp.minimum(i, half - 1), 0)),
            pl.BlockSpec((block, width), lambda i: (jnp.maximum(i - half, 0), 0)),
        ],
        out_specs=pl.BlockSpec((block, width), lambda i: (i, 0)),
        compiler_params=params(),
        name="mix",
    )(z, total, low, high)


def swap(x, axis, mask):
    return lax.ppermute(x, axis, [(i, i ^ mask) for i in range(lax.axis_size(axis))])


def per_device(queries, keys, values, rates, head_scale, w_one, w_three, w_two):
    tokens, width = queries.shape
    heads, size = w_one.shape[0], w_one.shape[1]
    devices = lax.axis_size("seq")
    place = lax.axis_index("seq")
    quarter = (place & 3).astype(jnp.int32).reshape(1)
    first = (place == 0).astype(jnp.int32).reshape(1)

    halo = lax.ppermute(tails(keys, values), "seq", [(i, i + 1) for i in range(devices - 1)])

    own, s1, s2, s3, wt = grads(quarter, keys, values, rates.T, w_one, w_three, w_two, 0, heads)
    r3, r1, r2 = swap(s3, "seq", 3), swap(s1, "seq", 1), swap(s2, "seq", 2)
    rows = own.shape[1]
    wire = jax.ShapeDtypeStruct((heads, rows + PAD, size), WIRE)
    mine = per_head(gather_body, wire, own, r1, r2, r3, name="gather")
    bit = 4
    while bit * 2 < devices:
        mine = per_head(cross_body, wire, mine, swap(mine, "seq", bit), name="cross")
        bit *= 2
    pieces = (mine, swap(mine, "seq", bit))
    new = per_head(
        renorm_body, wire, wt, *pieces, name="renorm", scalar=quarter
    )
    n3, n1, n2 = swap(new, "seq", 3), swap(new, "seq", 1), swap(new, "seq", 2)
    zed, local, new_t = apply(quarter, queries, head_scale, new, n1, n2, n3, 0)
    total = jnp.sum(local, axis=0)
    mask = 1
    while mask < lax.axis_size("head"):
        total = total + swap(total, "head", mask)
        mask *= 2
    square = jax.ShapeDtypeStruct((heads, size, size), F32)
    new_one, new_three, new_two = per_head(weights_body, (square, square, square), new_t, name="weights")

    blocks = tuple(range(tokens // 256))
    attn_high = attend(first, queries, keys, values, None, blocks[2:], size)
    attn_low = attend(first, queries, keys, values, halo, blocks[:2], size)
    features = heads * lax.axis_size("head") * size
    mixed = mix(zed, total, attn_low, attn_high, features)
    return (mixed, new_one, new_three, new_two)


def solution(mesh):
    placed = (
        P("seq", "head"),
        P("seq", "head"),
        P("seq", "head"),
        P("seq", "head"),
        P("head"),
        P("head", None, None),
        P("head", None, None),
        P("head", None, None),
    )
    return jax.shard_map(
        per_device,
        mesh=mesh,
        in_specs=placed,
        out_specs=(
            P("seq", "head"),
            P("head", None, None),
            P("head", None, None),
            P("head", None, None),
        ),
        check_vma=False,
    )
```

```python
import functools

import jax
import jax.numpy as jnp
from jax import lax
from jax.experimental import pallas as pl
from jax.experimental.pallas import tpu as pltpu
from jax.sharding import PartitionSpec as P


WINDOW_SPAN = 512
EPS = 1e-06
PAD = 16
KIND = 0
ORDERS = ((3, 1, 2), (2, 1, 3))
WIRE = jnp.bfloat16
REACH = 120.0
BF = jnp.bfloat16
F32 = jnp.float32


def params(mib=24):
    return pltpu.CompilerParams(vmem_limit_bytes=mib * 1024 * 1024)


VM = pl.BlockSpec(memory_space=pltpu.VMEM)
SM = pl.BlockSpec(memory_space=pltpu.SMEM)
FAR = pl.BlockSpec(memory_space=pltpu.HBM)


def call(body, outs, args, specs=None, away=False, scratch=(), flops=0):
    many = isinstance(outs, (tuple, list))
    listed = list(outs) if many else [outs]
    away = list(away) if isinstance(away, tuple) else [away] * len(listed)
    made = [pltpu.HBM(o.shape, o.dtype) if a else pltpu.VMEM(o.shape, o.dtype) for o, a in zip(listed, away)]
    places = [FAR if a else VM for a in away]
    return pl.pallas_call(
        body,
        out_shape=tuple(made) if many else made[0],
        in_specs=specs or [VM] * len(args),
        out_specs=tuple(places) if many else places[0],
        scratch_shapes=list(scratch),
        compiler_params=params(),
        cost_estimate=pl.CostEstimate(flops=flops or 1 << 24, bytes_accessed=1 << 21, transcendentals=0),
    )(*args)


def spec(shape, dtype):
    return jax.ShapeDtypeStruct(shape, dtype)


def nn(a, b):
    return lax.dot_general(a, b, (((1,), (0,)), ((), ())), preferred_element_type=F32)


def nt(a, b):
    return lax.dot_general(a, b, (((1,), (1,)), ((), ())), preferred_element_type=F32)


def split(x):
    high = x.astype(BF)
    return high, (x - high.astype(F32)).astype(BF)


def encode(x, ref):
    rows, size = x.shape
    top = jnp.max(jnp.abs(x), axis=1, keepdims=True)
    scale = (jnp.maximum(top, 1e-30) * 1.008).astype(WIRE).astype(F32)
    code = jnp.exp2(jnp.abs(x) * (2.0 * REACH / scale) - REACH)
    ref[0:rows] = jnp.where(x < 0, -code, code).astype(WIRE)
    column = jnp.concatenate([scale, jnp.zeros((size - rows, 1), F32)], axis=0)
    ref[rows : rows + PAD] = jnp.broadcast_to(column, (size, 128)).T[0:PAD].astype(WIRE)


def decode(ref):
    rows = ref.shape[0] - PAD
    scale = ref[rows : rows + PAD].astype(F32).T[0:rows, 0:1]
    code = ref[0:rows].astype(F32)
    size = (jnp.log2(jnp.abs(code)) + REACH) * (scale * (0.5 / REACH))
    return jnp.where(code < 0, -size, size)


def grads_body(quarter, q_far, k_far, v_far, r_far, w1_far, w3_far, w2_far, *refs):
    own_ref, p1_ref, p2_ref, p3_ref, mine_far, q_ref, k_ref, v_ref, *tails = refs[:-7]
    acc, part, r_ref, w1_ref, w3_ref, w2_ref, sems = refs[-7:]
    heads, size = w1_ref.shape[0], w1_ref.shape[1]
    tokens = k_ref.shape[0]
    step = min(256, tokens)
    count = tokens // step
    used = []

    def copy(source, target):
        made = pltpu.make_async_copy(source, target, sems.at[len(used)])
        made.start()
        used.append(made)
        return made

    def block(ref, index):
        return ref.at[index * step : (index + 1) * step]

    def fetch(index):
        return copy(block(k_far, index), block(k_ref, index)), copy(block(v_far, index), block(v_ref, index))

    first = [copy(w1_far, w1_ref)]
    coming = [fetch(0)]
    first += [copy(w3_far, w3_ref), copy(w2_far, w2_ref), copy(r_far, r_ref)]
    coming += [fetch(index) for index in range(1, count)]
    late = [copy(q_far, q_ref)]
    rows = 3 * size // 4
    q = quarter[0]
    own_rows = pl.ds(pl.multiple_of(q * rows, 8), rows)
    halves = []
    for made in first:
        made.wait()
    for head in range(heads):
        w1t, w3t, w2 = w1_ref[head].T, w3_ref[head].T, w2_ref[head]
        halves.append((*split(w1t), *split(w3t), *split(w2)))
        acc[0:size] = w1t
        acc[size : 2 * size] = w3t
        acc[2 * size : 3 * size] = w2.T
        part[head] = acc[own_rows]
        late.append(copy(part.at[head], mine_far.at[head]))
    sums = [None] * heads
    edge = tokens - WINDOW_SPAN
    for index in range(count):
        for made in coming[index]:
            made.wait()
        start = index * step
        if start >= edge:
            late.append(copy(block(v_ref, index), tails[(start - edge) // step]))
        for head in range(heads):
            w1h, w1l, w3h, w3l, w2h, w2l = halves[head]
            cols = slice(head * size, (head + 1) * size)
            kb = k_ref[start : start + step, cols]
            vb = v_ref[start : start + step, cols]
            rate = r_ref[head : head + 1, start : start + step]
            h1 = nt(w1h, kb) + nt(w1l, kb)
            h3 = nt(w3h, kb) + nt(w3l, kb)
            da = (nt(w2h, vb) + nt(w2l, vb)) * rate
            sg = 1.0 / (1.0 + jnp.exp(-h1))
            sil = h1 * sg
            act = sil * h3 * rate
            d3 = da * sil
            d1 = da * h3 * (sg * (1.0 + h1 * (1.0 - sg)))
            ah, al = split(act)
            d1h, d1l = split(d1)
            d3h, d3l = split(d3)
            new = (nn(d1h, kb) + nn(d1l, kb), nn(d3h, kb) + nn(d3l, kb), nn(ah, vb) + nn(al, vb))
            sums[head] = new if sums[head] is None else tuple(x + y for x, y in zip(sums[head], new))
    for head in range(heads):
        g1, g3, g2 = sums[head]
        acc[0:size] = g1
        acc[size : 2 * size] = g3
        acc[2 * size : 3 * size] = g2.T
        own_ref[head] = acc[own_rows]
        for j, ref in ((1, p1_ref), (2, p2_ref), (3, p3_ref)):
            encode(acc[pl.ds(pl.multiple_of((q ^ j) * rows, 8), rows)], ref.at[head])
    for made in late:
        made.wait()


def far(*args):
    return [pltpu.with_memory_space_constraint(a, pltpu.HBM) for a in args]


def near(*args):
    return [pltpu.with_memory_space_constraint(a, pltpu.VMEM) for a in args]


def grads(quarter, queries, keys, values, rates_t, w1, w3, w2):
    heads, size = w1.shape[0], w1.shape[1]
    rows = 3 * size // 4
    whole = pltpu.VMEM(w1.shape, F32)
    step = min(256, keys.shape[0])
    pieces = WINDOW_SPAN // step
    scratch = (
        pltpu.VMEM((3 * size, size), F32),
        pltpu.VMEM((heads, rows, size), F32),
        pltpu.VMEM(rates_t.shape, F32),
        whole,
        whole,
        whole,
        pltpu.SemaphoreType.DMA((4 + 2 * (keys.shape[0] // step) + 1 + heads + pieces,)),
    )
    wire = spec((heads, rows + PAD, size), WIRE)
    part = spec((heads, rows, size), F32)
    inputs = [spec(a.shape, a.dtype) for a in (queries, keys, values)]
    tail = spec((step, keys.shape[1]), keys.dtype)
    outs = (part, wire, wire, wire, part, *inputs, *[tail] * pieces)
    away = (False, False, False, False, True, False, False, False, *[True] * pieces)
    args = (quarter, *far(queries, keys, values, rates_t, w1, w3, w2))
    out = call(grads_body, outs, args, [SM] + [FAR] * 7, away, scratch, 1 << 31)
    return out[:8], out[8:]


def tail_body(k_far, out_ref, sems):
    edge = k_far.shape[0] - WINDOW_SPAN
    half = WINDOW_SPAN // 2
    copies = [
        pltpu.make_async_copy(k_far.at[edge + at : edge + at + half], out_ref.at[at : at + half], sems.at[at // half])
        for at in (0, half)
    ]
    for made in copies:
        made.start()
    for made in copies:
        made.wait()


def tail(keys):
    out = spec((WINDOW_SPAN, keys.shape[1]), keys.dtype)
    return call(tail_body, out, far(keys), [FAR], False, (pltpu.SemaphoreType.DMA((2,)),))


class Rows:
    def __init__(self, ref, head, size, step):
        self.ref, self.step, self.count = ref, step, ref.shape[0] // step
        self.cols = slice(head * size, (head + 1) * size)

    def at(self, index):
        return self.ref.at[index * self.step : (index + 1) * self.step, self.cols]

    def __call__(self, index):
        return self.ref[index * self.step : (index + 1) * self.step, self.cols]


def heads_of(ref):
    return range(ref.shape[0])


def gather_body(own_ref, r1_ref, r2_ref, r3_ref, out_ref):
    for h in heads_of(out_ref):
        pair = decode(r2_ref.at[h]) + decode(r3_ref.at[h])
        encode(own_ref[h] + decode(r1_ref.at[h]) + pair, out_ref.at[h])


def cross_body(mine_ref, other_ref, out_ref):
    for h in heads_of(out_ref):
        encode(decode(mine_ref.at[h]) + decode(other_ref.at[h]), out_ref.at[h])


def renorm_body(w_far, mine_ref, other_ref, out_ref, w_ref, sem):
    fetch = pltpu.make_async_copy(w_far, w_ref, sem)
    fetch.start()
    sums = [decode(mine_ref.at[h]) + decode(other_ref.at[h]) for h in heads_of(out_ref)]
    fetch.wait()
    for h, total in enumerate(sums):
        w = w_ref[h]
        upd = w + total
        old = jnp.sqrt(jnp.sum(w * w, axis=1, keepdims=True) + EPS)
        cur = jnp.sqrt(jnp.sum(upd * upd, axis=1, keepdims=True) + EPS)
        encode(upd * (old / cur), out_ref.at[h])


def apply_body(quarter, s_ref, q_ref, own_ref, r1_ref, r2_ref, r3_ref, z_ref, sq_ref, n_ref):
    heads, rows, size = own_ref.shape
    rows -= PAD
    tokens = q_ref.shape[0]
    q = quarter[0]
    block = min(256, tokens)
    for head in range(heads):
        for j, ref in enumerate((own_ref, r1_ref, r2_ref, r3_ref)):
            n_ref[head, pl.ds(pl.multiple_of((q ^ j) * rows, 8), rows)] = decode(ref.at[head])
        n1h, n1l = split(n_ref[head, 0:size])
        n3h, n3l = split(n_ref[head, size : 2 * size])
        n2h, n2l = split(n_ref[head, 2 * size : 3 * size])
        scale = s_ref[head]
        for start in range(0, tokens, block):
            qb = q_ref[start : start + block, head * size : (head + 1) * size]
            p1 = nt(qb, n1h) + nt(qb, n1l)
            p3 = nt(qb, n3h) + nt(qb, n3l)
            hh, hl = split(p1 * (1.0 / (1.0 + jnp.exp(-p1))) * p3)
            zed = (nt(hh, n2h) + nt(hl, n2h) + nt(hh, n2l)) * scale
            z_ref[start : start + block, head * size : (head + 1) * size] = zed
            zz = zed * zed
            half = zz[:, 0:128]
            for lane in range(128, size, 128):
                half = half + zz[:, lane : lane + 128]
            found = jnp.sum(half.T, axis=0, keepdims=True)
            if head == 0:
                sq_ref[:, start : start + block] = found
            else:
                sq_ref[:, start : start + block] += found


def apply(quarter, queries, scale, pieces):
    heads, _, size = pieces[0].shape
    tokens = queries.shape[0]
    outs = (spec((tokens, heads * size), F32), spec((1, tokens), F32), spec((heads, 3 * size, size), F32))
    args = (quarter, scale, queries, *pieces)
    return call(apply_body, outs, args, [SM, SM] + [VM] * 5, flops=1 << 31)


def weights_body(n_ref, o1, o3, o2, buf, sems):
    size = o1.shape[1]
    copies = []
    for head in heads_of(n_ref):
        for place, out in enumerate((o1, o3, o2)):
            index = 3 * head + place
            buf[index] = n_ref[head, place * size : (place + 1) * size].T
            made = pltpu.make_async_copy(buf.at[index], out.at[head], sems.at[index])
            made.start()
            copies.append(made)
    for made in copies:
        made.wait()


def weights(new):
    heads, _, size = new.shape
    square = spec((heads, size, size), F32)
    scratch = (pltpu.VMEM((3 * heads, size, size), F32), pltpu.SemaphoreType.DMA((3 * heads,)))
    return call(weights_body, (square,) * 3, (new,), away=True, scratch=scratch)


def attend_body(size, blocks, *refs):
    for head in range(refs[-1].shape[1] // size):
        attend_head(head, size, blocks, *refs)


def attend_head(head, size, blocks, first_ref, q_ref, k_ref, v_ref, *refs):
    halo = refs[:-1]
    out_ref = refs[-1]
    step = 256
    span = WINDOW_SPAN // step
    scale = size ** (-0.5)
    q, k, v = (Rows(ref, head, size, step) for ref in (q_ref, k_ref, v_ref))
    rows = lax.broadcasted_iota(jnp.int32, (step, step), 0)
    cols = lax.broadcasted_iota(jnp.int32, (step, step), 1)
    for place, block in enumerate(blocks):
        qb = q(block)
        scores, vals = [], []
        for back in range(span, -1, -1):
            source = block - back
            if source < 0:
                at = (source + span) * step
                kb, vb = halo[0][at : at + step, q.cols], halo[1 + at // step][:, q.cols]
            else:
                kb, vb = k(source), v(source)
            s = nt(qb, kb) * scale
            allowed = None
            if back == 0:
                allowed = cols <= rows
            if back == span:
                allowed = cols > rows
            if source < 0:
                here = first_ref[0] == 0
                allowed = here if allowed is None else allowed & here
            if allowed is not None:
                s = jnp.where(allowed, s, -jnp.inf)
            scores.append(s)
            vals.append(vb)
        top = scores[0].max(axis=-1, keepdims=True)
        for s in scores[1:]:
            top = jnp.maximum(top, s.max(axis=-1, keepdims=True))
        expo = [jnp.exp(s - top) for s in scores]
        total = expo[0].sum(axis=-1, keepdims=True)
        for x in expo[1:]:
            total = total + x.sum(axis=-1, keepdims=True)
        inverse = 1.0 / total
        out = None
        for x, vb in zip(expo, vals):
            part = nn((x * inverse).astype(BF), vb)
            out = part if out is None else out + part
        out_ref[place * step : (place + 1) * step, q.cols] = out


def attend(first, queries, keys, values, halo, blocks, size):
    args = (first, queries, keys, values) + (() if halo is None else tuple(halo))
    return call(
        functools.partial(attend_body, size, blocks),
        spec((len(blocks) * 256, queries.shape[1]), F32),
        args,
        [SM] + [VM] * (len(args) - 1),
        flops=1 << 30,
    )


def mix_body(features, r_ref, z_ref, a_ref, b_ref, out, buf, sems):
    tokens = buf.shape[0]
    step = 128
    half = tokens // 2
    inverse = 1.0 / jnp.sqrt(r_ref[...] / features + EPS)
    copies = []
    for index in range(tokens // step):
        start = index * step
        column = jnp.broadcast_to(inverse[:, start : start + step], (128, step)).T[:, 0:1]
        attn = a_ref[start : start + step] if start < half else b_ref[start - half : start - half + step]
        buf[start : start + step] = attn + z_ref[start : start + step] * column
        made = pltpu.make_async_copy(buf.at[start : start + step], out.at[start : start + step], sems.at[index])
        made.start()
        copies.append(made)
    for made in copies:
        made.wait()


def mix(total, z, low, high, features):
    scratch = (pltpu.VMEM(z.shape, F32), pltpu.SemaphoreType.DMA((z.shape[0] // 128,)))
    args = (total, z, low, high)
    return call(functools.partial(mix_body, features), spec(z.shape, F32), args, away=True, scratch=scratch)


def swap(x, axis, mask):
    return lax.ppermute(x, axis, [(i, i ^ mask) for i in range(lax.axis_size(axis))])


def after(x, *others):
    return lax.optimization_barrier((x, *others))[0]


def plan(place, devices, kind):
    bits = [(place >> n) & 1 for n in range(3)]
    rest = [1 << n for n in range(3, devices.bit_length() - 1)]
    if kind == 0:
        return bits[0] + 2 * (bits[1] ^ bits[2]), (1, 2, 3), ORDERS[0], [6, *rest]
    return bits[1] + 2 * bits[2], (2, 4, 6), ORDERS[1], [1, *rest]


def per_device(queries, keys, values, rates, head_scale, w_one, w_three, w_two):
    tokens, _ = queries.shape
    heads, size = w_one.shape[0], w_one.shape[1]
    rows = 3 * size // 4
    devices = lax.axis_size("seq")
    place = lax.axis_index("seq").astype(jnp.int32)
    first = (place == 0).astype(jnp.int32).reshape(1)
    blocks = tuple(range(tokens // 256))
    half = len(blocks) // 2
    wire = spec((heads, rows + PAD, size), WIRE)
    ring = [(i, (i + 1) % devices) for i in range(devices)]
    quarter, masks, order, shared = plan(place, devices, KIND)
    quarter = quarter.reshape(1)

    def spread(parts):
        out = {}
        for j in order:
            out[j] = near(swap(parts[j - 1], "seq", masks[j - 1]))[0]
        return out[1], out[2], out[3]

    halo = [lax.ppermute(tail(keys), "seq", ring)]
    out, ends = grads(quarter, queries, keys, values, rates.T, w_one, w_three, w_two)
    own, p1, p2, p3, mine_w, q, k, v = out
    got = spread((p1, p2, p3))
    halo.append(lax.ppermute(ends[0], "seq", ring))
    high = attend(first, q, k, v, None, blocks[half:], size)
    mine = call(gather_body, wire, (after(own, high), *got))
    for mask in shared[:-1]:
        mine = call(cross_body, wire, (mine, swap(mine, "seq", mask)))
    other = near(swap(mine, "seq", shared[-1]))[0]
    for place, end in enumerate(ends[1:], 1):
        halo.append(lax.ppermute(after(end, mine), "seq", ring))
    scratch = (pltpu.VMEM((heads, rows, size), F32), pltpu.SemaphoreType.DMA)
    new = call(renorm_body, wire, (mine_w, mine, other), [FAR, VM, VM], scratch=scratch)
    pieces = (new, *spread((new, new, new)))
    low = attend(first, q, after(k, new), v, halo, blocks[:half], size)
    pieces = (after(new, low), *pieces[1:])
    zed, total, new_t = apply(quarter, q, head_scale, pieces)
    mask = 1
    while mask < lax.axis_size("head"):
        total = total + swap(total, "head", mask)
        mask *= 2
    new_one, new_three, new_two = weights(new_t)
    mixed = mix(total, zed, low, high, heads * lax.axis_size("head") * size)
    return (mixed, new_one, new_three, new_two)


def solution(mesh):
    placed = (
        P("seq", "head"),
        P("seq", "head"),
        P("seq", "head"),
        P("seq", "head"),
        P("head"),
        P("head", None, None),
        P("head", None, None),
        P("head", None, None),
    )
    return jax.shard_map(
        per_device,
        mesh=mesh,
        in_specs=placed,
        out_specs=(
            P("seq", "head"),
            P("head", None, None),
            P("head", None, None),
            P("head", None, None),
        ),
        check_vma=False,
    )
```

```python
import functools

import jax
import jax.numpy as jnp
from jax import lax
from jax.experimental import pallas as pl
from jax.experimental.pallas import tpu as pltpu
from jax.sharding import PartitionSpec as P


WINDOW_SPAN = 512
EPS = 1e-06
PAD = 8
KIND = 0
ORDERS = ((1, 2, 3), (2, 1, 3))
WIRE = jnp.bfloat16
REACH = 120.0
BF = jnp.bfloat16
F32 = jnp.float32


def params(mib=24):
    return pltpu.CompilerParams(vmem_limit_bytes=mib * 1024 * 1024)


VM = pl.BlockSpec(memory_space=pltpu.VMEM)
SM = pl.BlockSpec(memory_space=pltpu.SMEM)
FAR = pl.BlockSpec(memory_space=pltpu.HBM)


def call(body, outs, args, specs=None, away=False, scratch=(), flops=0):
    many = isinstance(outs, (tuple, list))
    listed = list(outs) if many else [outs]
    away = list(away) if isinstance(away, tuple) else [away] * len(listed)
    made = [pltpu.HBM(o.shape, o.dtype) if a else pltpu.VMEM(o.shape, o.dtype) for o, a in zip(listed, away)]
    places = [FAR if a else VM for a in away]
    return pl.pallas_call(
        body,
        out_shape=tuple(made) if many else made[0],
        in_specs=specs or [VM] * len(args),
        out_specs=tuple(places) if many else places[0],
        scratch_shapes=list(scratch),
        compiler_params=params(),
        cost_estimate=pl.CostEstimate(flops=flops or 1 << 24, bytes_accessed=1 << 21, transcendentals=0),
    )(*args)


def spec(shape, dtype):
    return jax.ShapeDtypeStruct(shape, dtype)


def nn(a, b):
    return lax.dot_general(a, b, (((1,), (0,)), ((), ())), preferred_element_type=F32)


def nt(a, b):
    return lax.dot_general(a, b, (((1,), (1,)), ((), ())), preferred_element_type=F32)


def split(x):
    high = x.astype(BF)
    return high, (x - high.astype(F32)).astype(BF)


def encode(x, ref):
    rows, size = x.shape
    top = jnp.max(jnp.abs(x), axis=1, keepdims=True)
    scale = (jnp.maximum(top, 1e-30) * 1.008).astype(WIRE).astype(F32)
    code = jnp.exp2(jnp.abs(x) * (2.0 * REACH / scale) - REACH)
    ref[0:rows] = jnp.where(x < 0, -code, code).astype(WIRE)
    column = jnp.concatenate([scale, jnp.zeros((size - rows, 1), F32)], axis=0)
    ref[rows : rows + PAD] = jnp.broadcast_to(column, (size, 128)).T[0:PAD].astype(WIRE)


def decode(ref):
    rows = ref.shape[0] - PAD
    scale = ref[rows : rows + PAD].astype(F32).T[0:rows, 0:1]
    code = ref[0:rows].astype(F32)
    size = (jnp.log2(jnp.abs(code)) + REACH) * (scale * (0.5 / REACH))
    return jnp.where(code < 0, -size, size)


def grads_body(quarter, q_far, k_far, v_far, r_far, w1_far, w3_far, w2_far, *refs):
    own_far, *wires, mine_far, q_ref, k_ref, v_ref, low_far, high_far = refs[:-9]
    acc, part, sent, wire, r_ref, w1_ref, w3_ref, w2_ref, sems = refs[-9:]
    heads, size = w1_ref.shape[0], w1_ref.shape[1]
    tokens = k_ref.shape[0]
    step = min(256, tokens)
    count = tokens // step
    used = []

    def copy(source, target):
        made = pltpu.make_async_copy(source, target, sems.at[len(used)])
        made.start()
        used.append(made)
        return made

    def block(ref, index):
        return ref.at[index * step : (index + 1) * step]

    def fetch(index):
        return copy(block(k_far, index), block(k_ref, index)), copy(block(v_far, index), block(v_ref, index))

    def weights_of(head):
        return [copy(a.at[head], b.at[head]) for a, b in ((w1_far, w1_ref), (w3_far, w3_ref), (w2_far, w2_ref))]

    first = [weights_of(0)]
    coming = [fetch(0)]
    rates = copy(r_far, r_ref)
    coming += [fetch(later) for later in range(1, count)]
    late = []
    rows = 3 * size // 4
    q = quarter[0]
    own_rows = pl.ds(pl.multiple_of(q * rows, 8), rows)
    edge = tokens - WINDOW_SPAN
    for head in range(heads):
        for made in first[head]:
            made.wait()
        w1t, w3t, w2 = w1_ref[head].T, w3_ref[head].T, w2_ref[head]
        w1h, w1l = split(w1t)
        w3h, w3l = split(w3t)
        w2h, w2l = split(w2)
        acc[0:size] = w1t
        acc[size : 2 * size] = w3t
        acc[2 * size : 3 * size] = w2.T
        part[head] = acc[own_rows]
        late.append(copy(part.at[head], mine_far.at[head]))
        g1 = g3 = g2 = None
        cols = slice(head * size, (head + 1) * size)
        for index in range(count):
            if head == 0:
                for made in coming[index]:
                    made.wait()
                if index == 0:
                    rates.wait()
                    first += [weights_of(later) for later in range(1, heads)]
                    late.append(copy(q_far, q_ref))
            start = index * step
            kb = k_ref[start : start + step, cols]
            vb = v_ref[start : start + step, cols]
            rate = r_ref[head : head + 1, start : start + step]
            h1 = nt(w1h, kb) + nt(w1l, kb)
            h3 = nt(w3h, kb) + nt(w3l, kb)
            da = (nt(w2h, vb) + nt(w2l, vb)) * rate
            sg = 1.0 / (1.0 + jnp.exp(-h1))
            sil = h1 * sg
            act = sil * h3 * rate
            d3 = da * sil
            d1 = da * h3 * (sg * (1.0 + h1 * (1.0 - sg)))
            ah, al = split(act)
            d1h, d1l = split(d1)
            d3h, d3l = split(d3)
            t1 = nn(d1h, kb) + nn(d1l, kb)
            t3 = nn(d3h, kb) + nn(d3l, kb)
            t2 = nn(ah, vb) + nn(al, vb)
            g1 = t1 if g1 is None else g1 + t1
            g3 = t3 if g3 is None else g3 + t3
            g2 = t2 if g2 is None else g2 + t2
        if head == 0:
            middle = edge + WINDOW_SPAN // 2
            late.append(copy(v_ref.at[middle:], low_far))
            late.append(copy(v_ref.at[edge:middle], high_far))
        acc[0:size] = g1
        acc[size : 2 * size] = g3
        acc[2 * size : 3 * size] = g2.T
        for j, far_ref in enumerate(wires, 1):
            encode(acc[pl.ds(pl.multiple_of((q ^ j) * rows, 8), rows)], wire.at[head, j - 1])
            late.append(copy(wire.at[head, j - 1], far_ref.at[head]))
        sent[head] = acc[own_rows]
        late.append(copy(sent.at[head], own_far.at[head]))
    for made in late:
        made.wait()


def far(*args):
    return [pltpu.with_memory_space_constraint(a, pltpu.HBM) for a in args]


def near(*args):
    return [pltpu.with_memory_space_constraint(a, pltpu.VMEM) for a in args]


def grads(quarter, queries, keys, values, rates_t, w1, w3, w2):
    heads, size = w1.shape[0], w1.shape[1]
    rows = 3 * size // 4
    whole = pltpu.VMEM(w1.shape, F32)
    step = min(256, keys.shape[0])
    copies = 1 + 3 * heads + 2 * (keys.shape[0] // step) + 1 + 5 * heads + 2
    scratch = (
        pltpu.VMEM((3 * size, size), F32),
        pltpu.VMEM((heads, rows, size), F32),
        pltpu.VMEM((heads, rows, size), F32),
        pltpu.VMEM((heads, 3, rows + PAD, size), WIRE),
        pltpu.VMEM(rates_t.shape, F32),
        whole,
        whole,
        whole,
        pltpu.SemaphoreType.DMA((copies,)),
    )
    wire = spec((heads, rows + PAD, size), WIRE)
    part = spec((heads, rows, size), F32)
    inputs = [spec(a.shape, a.dtype) for a in (queries, keys, values)]
    half = (WINDOW_SPAN // 2, keys.shape[1])
    outs = (part, wire, wire, wire, part, *inputs, spec(half, keys.dtype), spec(half, keys.dtype))
    away = (True, True, True, True, True, False, False, False, True, True)
    args = (quarter, *far(queries, keys, values, rates_t, w1, w3, w2))
    return call(grads_body, outs, args, [SM] + [FAR] * 7, away, scratch, 1 << 31)


def tail_body(k_far, out_ref, sem):
    made = pltpu.make_async_copy(k_far.at[k_far.shape[0] - out_ref.shape[0] :], out_ref, sem)
    made.start()
    made.wait()


def tail(keys):
    out = spec((WINDOW_SPAN, keys.shape[1]), keys.dtype)
    return call(tail_body, out, far(keys), [FAR], False, (pltpu.SemaphoreType.DMA,))


class Rows:
    def __init__(self, ref, head, size, step):
        self.ref, self.step, self.count = ref, step, ref.shape[0] // step
        self.cols = slice(head * size, (head + 1) * size)

    def at(self, index):
        return self.ref.at[index * self.step : (index + 1) * self.step, self.cols]

    def __call__(self, index):
        return self.ref[index * self.step : (index + 1) * self.step, self.cols]


def heads_of(ref):
    return range(ref.shape[0])


def gather_body(own_ref, r1_ref, r2_ref, r3_ref, out_ref):
    for h in heads_of(out_ref):
        pair = decode(r2_ref.at[h]) + decode(r3_ref.at[h])
        encode(own_ref[h] + decode(r1_ref.at[h]) + pair, out_ref.at[h])


def cross_body(mine_ref, other_ref, out_ref):
    for h in heads_of(out_ref):
        encode(decode(mine_ref.at[h]) + decode(other_ref.at[h]), out_ref.at[h])


def renorm_body(w_far, mine_ref, other_ref, out_ref, w_ref, sem):
    fetch = pltpu.make_async_copy(w_far, w_ref, sem)
    fetch.start()
    sums = [decode(mine_ref.at[h]) + decode(other_ref.at[h]) for h in heads_of(out_ref)]
    fetch.wait()
    for h, total in enumerate(sums):
        w = w_ref[h]
        upd = w + total
        old = jnp.sqrt(jnp.sum(w * w, axis=1, keepdims=True) + EPS)
        cur = jnp.sqrt(jnp.sum(upd * upd, axis=1, keepdims=True) + EPS)
        encode(upd * (old / cur), out_ref.at[h])


def apply_body(quarter, s_ref, q_ref, own_ref, r1_ref, r2_ref, r3_ref, z_ref, sq_ref, n_ref):
    heads, rows, size = own_ref.shape
    rows -= PAD
    tokens = q_ref.shape[0]
    q = quarter[0]
    block = min(256, tokens)
    for head in range(heads):
        for j, ref in enumerate((own_ref, r1_ref, r2_ref, r3_ref)):
            n_ref[head, pl.ds(pl.multiple_of((q ^ j) * rows, 8), rows)] = decode(ref.at[head])
        n1h, n1l = split(n_ref[head, 0:size])
        n3h, n3l = split(n_ref[head, size : 2 * size])
        n2h, n2l = split(n_ref[head, 2 * size : 3 * size])
        scale = s_ref[head]
        for start in range(0, tokens, block):
            qb = q_ref[start : start + block, head * size : (head + 1) * size]
            p1 = nt(qb, n1h) + nt(qb, n1l)
            p3 = nt(qb, n3h) + nt(qb, n3l)
            hh, hl = split(p1 * (1.0 / (1.0 + jnp.exp(-p1))) * p3)
            zed = (nt(hh, n2h) + nt(hl, n2h) + nt(hh, n2l)) * scale
            z_ref[start : start + block, head * size : (head + 1) * size] = zed
            zz = zed * zed
            half = zz[:, 0:128]
            for lane in range(128, size, 128):
                half = half + zz[:, lane : lane + 128]
            found = jnp.sum(half.T, axis=0, keepdims=True)
            if head == 0:
                sq_ref[:, start : start + block] = found
            else:
                sq_ref[:, start : start + block] += found


def apply(quarter, queries, scale, pieces):
    heads, _, size = pieces[0].shape
    tokens = queries.shape[0]
    outs = (spec((tokens, heads * size), F32), spec((1, tokens), F32), spec((heads, 3 * size, size), F32))
    args = (quarter, scale, queries, *pieces)
    return call(apply_body, outs, args, [SM, SM] + [VM] * 5, flops=1 << 31)


def weights_body(n_ref, o1, o3, o2, buf, sems):
    size = o1.shape[1]
    copies = []
    for head in heads_of(n_ref):
        for place, out in enumerate((o1, o3, o2)):
            index = 3 * head + place
            buf[index] = n_ref[head, place * size : (place + 1) * size].T
            made = pltpu.make_async_copy(buf.at[index], out.at[head], sems.at[index])
            made.start()
            copies.append(made)
    for made in copies:
        made.wait()


def weights(new):
    heads, _, size = new.shape
    square = spec((heads, size, size), F32)
    scratch = (pltpu.VMEM((3 * heads, size, size), F32), pltpu.SemaphoreType.DMA((3 * heads,)))
    return call(weights_body, (square,) * 3, (new,), away=True, scratch=scratch)


def attend_body(size, blocks, *refs):
    for head in range(refs[-1].shape[1] // size):
        attend_head(head, size, blocks, *refs)


def attend_head(head, size, blocks, first_ref, q_ref, k_ref, v_ref, *refs):
    halo = refs[:-1]
    out_ref = refs[-1]
    step = 256
    span = WINDOW_SPAN // step
    scale = size ** (-0.5)
    q, k, v = (Rows(ref, head, size, step) for ref in (q_ref, k_ref, v_ref))
    rows = lax.broadcasted_iota(jnp.int32, (step, step), 0)
    cols = lax.broadcasted_iota(jnp.int32, (step, step), 1)
    for place, block in enumerate(blocks):
        qb = q(block)
        scores, vals = [], []
        for back in range(span, -1, -1):
            source = block - back
            if source < 0:
                at = (source + span) * step
                kb, vb = halo[0][at : at + step, q.cols], halo[span - at // step][:, q.cols]
            else:
                kb, vb = k(source), v(source)
            s = nt(qb, kb) * scale
            allowed = None
            if back == 0:
                allowed = cols <= rows
            if back == span:
                allowed = cols > rows
            if source < 0:
                here = first_ref[0] == 0
                allowed = here if allowed is None else allowed & here
            if allowed is not None:
                s = jnp.where(allowed, s, -jnp.inf)
            scores.append(s)
            vals.append(vb)
        top = scores[0].max(axis=-1, keepdims=True)
        for s in scores[1:]:
            top = jnp.maximum(top, s.max(axis=-1, keepdims=True))
        expo = [jnp.exp(s - top) for s in scores]
        total = expo[0].sum(axis=-1, keepdims=True)
        for x in expo[1:]:
            total = total + x.sum(axis=-1, keepdims=True)
        inverse = 1.0 / total
        out = None
        for x, vb in zip(expo, vals):
            part = nn((x * inverse).astype(BF), vb)
            out = part if out is None else out + part
        out_ref[place * step : (place + 1) * step, q.cols] = out


def attend(first, queries, keys, values, halo, blocks, size):
    args = (first, queries, keys, values) + (() if halo is None else tuple(halo))
    return call(
        functools.partial(attend_body, size, blocks),
        spec((len(blocks) * 256, queries.shape[1]), F32),
        args,
        [SM] + [VM] * (len(args) - 1),
        flops=1 << 30,
    )


def mix_body(features, r_ref, z_ref, *refs):
    *parts, out, buf, sems = refs
    tokens = buf.shape[0]
    step = 128
    attended = [(ref, at) for ref in parts for at in range(0, ref.shape[0], step)]
    inverse = 1.0 / jnp.sqrt(r_ref[...] / features + EPS)
    copies = []
    for index in range(tokens // step):
        start = index * step
        column = jnp.broadcast_to(inverse[:, start : start + step], (128, step)).T[:, 0:1]
        ref, at = attended[index]
        buf[start : start + step] = ref[at : at + step] + z_ref[start : start + step] * column
        made = pltpu.make_async_copy(buf.at[start : start + step], out.at[start : start + step], sems.at[index])
        made.start()
        copies.append(made)
    for made in copies:
        made.wait()


def mix(total, z, *parts, features):
    scratch = (pltpu.VMEM(z.shape, F32), pltpu.SemaphoreType.DMA((z.shape[0] // 128,)))
    args = (total, z, *parts)
    return call(functools.partial(mix_body, features), spec(z.shape, F32), args, away=True, scratch=scratch)


def swap(x, axis, mask):
    return lax.ppermute(x, axis, [(i, i ^ mask) for i in range(lax.axis_size(axis))])


def after(x, *others):
    return lax.optimization_barrier((x, *others))[0]


def plan(place, devices, kind):
    bits = [(place >> n) & 1 for n in range(3)]
    rest = [1 << n for n in range(3, devices.bit_length() - 1)]
    if kind == 0:
        return bits[0] + 2 * (bits[1] ^ bits[2]), (1, 2, 3), ORDERS[0], [6, *rest]
    return bits[1] + 2 * bits[2], (2, 4, 6), ORDERS[1], [1, *rest]


def per_device(queries, keys, values, rates, head_scale, w_one, w_three, w_two):
    tokens, _ = queries.shape
    heads, size = w_one.shape[0], w_one.shape[1]
    rows = 3 * size // 4
    devices = lax.axis_size("seq")
    place = lax.axis_index("seq").astype(jnp.int32)
    first = (place == 0).astype(jnp.int32).reshape(1)
    blocks = tuple(range(tokens // 256))
    half = len(blocks) // 2
    wire = spec((heads, rows + PAD, size), WIRE)
    line = [(i, i + 1) for i in range(devices - 1)]
    ring = [*line, (devices - 1, 0)]
    quarter, masks, order, shared = plan(place, devices, KIND)
    quarter = quarter.reshape(1)

    def spread(parts):
        out = {}
        for j in order:
            out[j] = swap(parts[j - 1], "seq", masks[j - 1])
        return out[1], out[2], out[3]

    halo = [lax.ppermute(tail(keys), "seq", ring)]
    out = grads(quarter, queries, keys, values, rates.T, w_one, w_three, w_two)
    own, p1, p2, p3, mine_w, q, k, v, end, rest = out
    got = spread((p1, p2, p3))
    high = attend(first, q, k, v, None, blocks[half:], size)
    mine = call(gather_body, wire, (after(own, high), *got))
    for mask in shared[:-1]:
        mine = call(cross_body, wire, (mine, swap(mine, "seq", mask)))
    other = near(swap(mine, "seq", shared[-1]))[0]
    halo.append(lax.ppermute(after(end, mine), "seq", line))
    scratch = (pltpu.VMEM((heads, rows, size), F32), pltpu.SemaphoreType.DMA)
    new = call(renorm_body, wire, (mine_w, mine, other), [FAR, VM, VM], scratch=scratch)
    pieces = (new, *spread((new, new, new)))
    halo.append(lax.ppermute(after(rest, *pieces), "seq", ring))
    low1 = attend(first, q, after(k, new), v, halo[:2], blocks[1:half], size)
    pieces = (after(new, low1), *pieces[1:])
    zed, total, new_t = apply(quarter, q, head_scale, pieces)
    low0 = attend(first, q, after(k, new_t), v, halo, blocks[:1], size)
    mask = 1
    while mask < lax.axis_size("head"):
        total = total + swap(total, "head", mask)
        mask *= 2
    new_one, new_three, new_two = weights(new_t)
    mixed = mix(total, zed, low0, low1, high, features=heads * lax.axis_size("head") * size)
    return (mixed, new_one, new_three, new_two)


def solution(mesh):
    placed = (
        P("seq", "head"),
        P("seq", "head"),
        P("seq", "head"),
        P("seq", "head"),
        P("head"),
        P("head", None, None),
        P("head", None, None),
        P("head", None, None),
    )
    return jax.shard_map(
        per_device,
        mesh=mesh,
        in_specs=placed,
        out_specs=(
            P("seq", "head"),
            P("head", None, None),
            P("head", None, None),
            P("head", None, None),
        ),
        check_vma=False,
    )
```

```python
import functools

import jax
import jax.numpy as jnp
from jax import lax
from jax.experimental import pallas as pl
from jax.experimental.pallas import tpu as pltpu
from jax.sharding import PartitionSpec as P


WINDOW_SPAN = 512
EPS = 1e-06
PAD = 8
CUT = 128
KIND = 0
ORDERS = ((1, 2, 3), (2, 1, 3))
WIRE = jnp.bfloat16
REACH = 120.0
BF = jnp.bfloat16
F32 = jnp.float32


def params(mib=24):
    return pltpu.CompilerParams(vmem_limit_bytes=mib * 1024 * 1024)


VM = pl.BlockSpec(memory_space=pltpu.VMEM)
SM = pl.BlockSpec(memory_space=pltpu.SMEM)
FAR = pl.BlockSpec(memory_space=pltpu.HBM)


def call(body, outs, args, specs=None, away=False, scratch=(), flops=0):
    many = isinstance(outs, (tuple, list))
    listed = list(outs) if many else [outs]
    away = list(away) if isinstance(away, tuple) else [away] * len(listed)
    made = [pltpu.HBM(o.shape, o.dtype) if a else pltpu.VMEM(o.shape, o.dtype) for o, a in zip(listed, away)]
    places = [FAR if a else VM for a in away]
    return pl.pallas_call(
        body,
        out_shape=tuple(made) if many else made[0],
        in_specs=specs or [VM] * len(args),
        out_specs=tuple(places) if many else places[0],
        scratch_shapes=list(scratch),
        compiler_params=params(),
        cost_estimate=pl.CostEstimate(flops=flops or 1 << 24, bytes_accessed=1 << 21, transcendentals=0),
    )(*args)


def spec(shape, dtype):
    return jax.ShapeDtypeStruct(shape, dtype)


def nn(a, b):
    return lax.dot_general(a, b, (((1,), (0,)), ((), ())), preferred_element_type=F32)


def nt(a, b):
    return lax.dot_general(a, b, (((1,), (1,)), ((), ())), preferred_element_type=F32)


def split(x):
    high = x.astype(BF)
    return high, (x - high.astype(F32)).astype(BF)


def encode(x, ref):
    rows, size = x.shape
    top = jnp.max(jnp.abs(x), axis=1, keepdims=True)
    scale = (jnp.maximum(top, 1e-30) * 1.008).astype(WIRE).astype(F32)
    code = jnp.exp2(jnp.abs(x) * (2.0 * REACH / scale) - REACH)
    ref[0:rows] = jnp.where(x < 0, -code, code).astype(WIRE)
    column = jnp.concatenate([scale, jnp.zeros((size - rows, 1), F32)], axis=0)
    ref[rows : rows + PAD] = jnp.broadcast_to(column, (size, 128)).T[0:PAD].astype(WIRE)


def decode(ref):
    rows = ref.shape[0] - PAD
    scale = ref[rows : rows + PAD].astype(F32).T[0:rows, 0:1]
    code = ref[0:rows].astype(F32)
    size = (jnp.log2(jnp.abs(code)) + REACH) * (scale * (0.5 / REACH))
    return jnp.where(code < 0, -size, size)


def grads_body(quarter, q_far, k_far, v_far, r_far, w1_far, w3_far, w2_far, *refs):
    own_far, *wires, mine_far, q_ref, k_ref, v_ref, low_far, high_far, mid_far = refs[:-9]
    acc, part, sent, wire, r_ref, w1_ref, w3_ref, w2_ref, sems = refs[-9:]
    heads, size = w1_ref.shape[0], w1_ref.shape[1]
    tokens = k_ref.shape[0]
    step = min(256, tokens)
    count = tokens // step
    used = []

    def copy(source, target):
        made = pltpu.make_async_copy(source, target, sems.at[len(used)])
        made.start()
        used.append(made)
        return made

    def block(ref, index):
        return ref.at[index * step : (index + 1) * step]

    def fetch(index):
        return copy(block(k_far, index), block(k_ref, index)), copy(block(v_far, index), block(v_ref, index))

    def weights_of(head):
        return [copy(a.at[head], b.at[head]) for a, b in ((w1_far, w1_ref), (w3_far, w3_ref), (w2_far, w2_ref))]

    first = [weights_of(0)]
    coming = [fetch(0)]
    rates = copy(r_far, r_ref)
    coming += [fetch(later) for later in range(1, count)]
    late = []
    rows = 3 * size // 4
    q = quarter[0]
    own_rows = pl.ds(pl.multiple_of(q * rows, 8), rows)
    edge = tokens - WINDOW_SPAN
    for head in range(heads):
        first[head][0].wait()
        w1t = w1_ref[head].T
        w1h, w1l = split(w1t)
        first[head][1].wait()
        w3t = w3_ref[head].T
        w3h, w3l = split(w3t)
        first[head][2].wait()
        w2 = w2_ref[head]
        w2h, w2l = split(w2)
        acc[0:size] = w1t
        acc[size : 2 * size] = w3t
        acc[2 * size : 3 * size] = w2.T
        part[head] = acc[own_rows]
        late.append(copy(part.at[head], mine_far.at[head]))
        g1 = g3 = g2 = None
        cols = slice(head * size, (head + 1) * size)
        for index in range(count):
            if head == 0:
                for made in coming[index]:
                    made.wait()
                if index == 0:
                    rates.wait()
                    first += [weights_of(later) for later in range(1, heads)]
                    late.append(copy(q_far, q_ref))
            start = index * step
            kb = k_ref[start : start + step, cols]
            vb = v_ref[start : start + step, cols]
            rate = r_ref[head : head + 1, start : start + step]
            kk = jnp.concatenate([kb, kb], axis=1)
            h1 = nt(jnp.concatenate([w1h, w1l], axis=1), kk)
            h3 = nt(jnp.concatenate([w3h, w3l], axis=1), kk)
            da = nt(jnp.concatenate([w2h, w2l], axis=1), jnp.concatenate([vb, vb], axis=1)) * rate
            sg = 1.0 / (1.0 + jnp.exp(-h1))
            sil = h1 * sg
            act = sil * h3 * rate
            d3 = da * sil
            d1 = da * h3 * (sg * (1.0 + h1 * (1.0 - sg)))
            ah, al = split(act)
            d1h, d1l = split(d1)
            d3h, d3l = split(d3)
            kk = jnp.concatenate([kb, kb], axis=0)
            t1 = nn(jnp.concatenate([d1h, d1l], axis=1), kk)
            t3 = nn(jnp.concatenate([d3h, d3l], axis=1), kk)
            t2 = nn(jnp.concatenate([ah, al], axis=1), jnp.concatenate([vb, vb], axis=0))
            g1 = t1 if g1 is None else g1 + t1
            g3 = t3 if g3 is None else g3 + t3
            g2 = t2 if g2 is None else g2 + t2
        if head == 0:
            middle = edge + WINDOW_SPAN // 2
            late.append(copy(k_ref.at[edge : edge + CUT], mid_far))
            late.append(copy(v_ref.at[middle:], low_far))
            late.append(copy(v_ref.at[edge:middle], high_far))
        acc[0:size] = g1
        acc[size : 2 * size] = g3
        acc[2 * size : 3 * size] = g2.T
        for j, far_ref in enumerate(wires, 1):
            encode(acc[pl.ds(pl.multiple_of((q ^ j) * rows, 8), rows)], wire.at[head, j - 1])
            late.append(copy(wire.at[head, j - 1], far_ref.at[head]))
        sent[head] = acc[own_rows]
        late.append(copy(sent.at[head], own_far.at[head]))
    for made in late:
        made.wait()


def far(*args):
    return [pltpu.with_memory_space_constraint(a, pltpu.HBM) for a in args]


def near(*args):
    return [pltpu.with_memory_space_constraint(a, pltpu.VMEM) for a in args]


def grads(quarter, queries, keys, values, rates_t, w1, w3, w2):
    heads, size = w1.shape[0], w1.shape[1]
    rows = 3 * size // 4
    whole = pltpu.VMEM(w1.shape, F32)
    step = min(256, keys.shape[0])
    copies = 1 + 3 * heads + 2 * (keys.shape[0] // step) + 1 + 5 * heads + 3
    scratch = (
        pltpu.VMEM((3 * size, size), F32),
        pltpu.VMEM((heads, rows, size), F32),
        pltpu.VMEM((heads, rows, size), F32),
        pltpu.VMEM((heads, 3, rows + PAD, size), WIRE),
        pltpu.VMEM(rates_t.shape, F32),
        whole,
        whole,
        whole,
        pltpu.SemaphoreType.DMA((copies,)),
    )
    wire = spec((heads, rows + PAD, size), WIRE)
    part = spec((heads, rows, size), F32)
    inputs = [spec(a.shape, a.dtype) for a in (queries, keys, values)]
    half = (WINDOW_SPAN // 2, keys.shape[1])
    outs = (part, wire, wire, wire, part, *inputs, spec(half, keys.dtype), spec(half, keys.dtype), spec((CUT, keys.shape[1]), keys.dtype))
    away = (True, True, True, True, True, False, False, False, True, True, True)
    args = (quarter, *far(queries, keys, values, rates_t, w1, w3, w2))
    return call(grads_body, outs, args, [SM] + [FAR] * 7, away, scratch, 1 << 31)


def tail_body(k_far, out_ref, sem):
    made = pltpu.make_async_copy(k_far.at[k_far.shape[0] - out_ref.shape[0] :], out_ref, sem)
    made.start()
    made.wait()


def tail(keys):
    out = spec((WINDOW_SPAN - CUT, keys.shape[1]), keys.dtype)
    return call(tail_body, out, far(keys), [FAR], False, (pltpu.SemaphoreType.DMA,))


class Rows:
    def __init__(self, ref, head, size, step):
        self.ref, self.step, self.count = ref, step, ref.shape[0] // step
        self.cols = slice(head * size, (head + 1) * size)

    def at(self, index):
        return self.ref.at[index * self.step : (index + 1) * self.step, self.cols]

    def __call__(self, index):
        return self.ref[index * self.step : (index + 1) * self.step, self.cols]


def heads_of(ref):
    return range(ref.shape[0])


def gather_body(own_ref, r1_ref, r2_ref, r3_ref, out_ref):
    for h in heads_of(out_ref):
        pair = decode(r2_ref.at[h]) + decode(r3_ref.at[h])
        encode(own_ref[h] + decode(r1_ref.at[h]) + pair, out_ref.at[h])


def cross_body(mine_ref, other_ref, out_ref):
    for h in heads_of(out_ref):
        encode(decode(mine_ref.at[h]) + decode(other_ref.at[h]), out_ref.at[h])


def renorm_body(w_far, mine_ref, other_ref, out_ref, w_ref, sem):
    fetch = pltpu.make_async_copy(w_far, w_ref, sem)
    fetch.start()
    sums = [decode(mine_ref.at[h]) + decode(other_ref.at[h]) for h in heads_of(out_ref)]
    fetch.wait()
    for h, total in enumerate(sums):
        w = w_ref[h]
        upd = w + total
        old = jnp.sqrt(jnp.sum(w * w, axis=1, keepdims=True) + EPS)
        cur = jnp.sqrt(jnp.sum(upd * upd, axis=1, keepdims=True) + EPS)
        encode(upd * (old / cur), out_ref.at[h])


def apply_body(quarter, s_ref, q_ref, own_ref, r1_ref, r2_ref, r3_ref, z_ref, sq_ref, n_ref):
    heads, rows, size = own_ref.shape
    rows -= PAD
    tokens = q_ref.shape[0]
    q = quarter[0]
    block = min(1024, tokens)
    for head in range(heads):
        for j, ref in enumerate((own_ref, r1_ref, r2_ref, r3_ref)):
            n_ref[head, pl.ds(pl.multiple_of((q ^ j) * rows, 8), rows)] = decode(ref.at[head])
        n1h, n1l = split(n_ref[head, 0:size])
        n3h, n3l = split(n_ref[head, size : 2 * size])
        n2h, n2l = split(n_ref[head, 2 * size : 3 * size])
        scale = s_ref[head]
        for start in range(0, tokens, block):
            qb = q_ref[start : start + block, head * size : (head + 1) * size]
            qq = jnp.concatenate([qb, qb], axis=1)
            p1 = nt(qq, jnp.concatenate([n1h, n1l], axis=1))
            p3 = nt(qq, jnp.concatenate([n3h, n3l], axis=1))
            hh, hl = split(p1 * (1.0 / (1.0 + jnp.exp(-p1))) * p3)
            zed = nt(jnp.concatenate([hh, hl, hh], axis=1), jnp.concatenate([n2h, n2h, n2l], axis=1)) * scale
            z_ref[start : start + block, head * size : (head + 1) * size] = zed
            zz = zed * zed
            half = zz[:, 0:128]
            for lane in range(128, size, 128):
                half = half + zz[:, lane : lane + 128]
            found = jnp.sum(half.T, axis=0, keepdims=True)
            if head == 0:
                sq_ref[:, start : start + block] = found
            else:
                sq_ref[:, start : start + block] += found


def apply(quarter, queries, scale, pieces):
    heads, _, size = pieces[0].shape
    tokens = queries.shape[0]
    outs = (spec((tokens, heads * size), F32), spec((1, tokens), F32), spec((heads, 3 * size, size), F32))
    args = (quarter, scale, queries, *pieces)
    return call(apply_body, outs, args, [SM, SM] + [VM] * 5, flops=1 << 31)


def weights_body(n_ref, o1, o3, o2, buf, sems):
    size = o1.shape[1]
    copies = []
    for head in heads_of(n_ref):
        for place, out in enumerate((o1, o3, o2)):
            index = 3 * head + place
            buf[index] = n_ref[head, place * size : (place + 1) * size].T
            made = pltpu.make_async_copy(buf.at[index], out.at[head], sems.at[index])
            made.start()
            copies.append(made)
    for made in copies:
        made.wait()


def weights(new):
    heads, _, size = new.shape
    square = spec((heads, size, size), F32)
    scratch = (pltpu.VMEM((3 * heads, size, size), F32), pltpu.SemaphoreType.DMA((3 * heads,)))
    return call(weights_body, (square,) * 3, (new,), away=True, scratch=scratch)


def attend_body(heads, size, blocks, *refs):
    for head in range(heads):
        attend_head(head, size, blocks, *refs)


def attend_head(head, size, blocks, first_ref, q_ref, k_ref, v_ref, *refs):
    early, part, mid = refs[:3] if len(refs) > 1 else (None, None, None)
    out_ref, probs_ref = (refs[3], refs[4]) if len(refs) > 1 else (refs[0], None)
    step = 256
    span = WINDOW_SPAN // step
    scale = size ** (-0.5)
    q, k, v = (Rows(ref, head, size, step) for ref in (q_ref, k_ref, v_ref))
    rows = lax.broadcasted_iota(jnp.int32, (step, step), 0)
    cols = lax.broadcasted_iota(jnp.int32, (step, step), 1)
    for place, block in enumerate(blocks):
        qb = q(block)
        scores, vals = [], []
        for back in range(span, -1, -1):
            source = block - back
            if source < 0:
                at = (source + span) * step
                if at == 0:
                    kb, vb = jnp.concatenate([part[:, q.cols], early[0 : step - CUT, q.cols]], axis=0), None
                else:
                    kb, vb = early[at - CUT : at - CUT + step, q.cols], mid[:, q.cols]
            else:
                kb, vb = k(source), v(source)
            s = nt(qb, kb) * scale
            allowed = None
            if back == 0:
                allowed = cols <= rows
            if back == span:
                allowed = cols > rows
            if source < 0:
                here = first_ref[0] == 0
                allowed = here if allowed is None else allowed & here
            if allowed is not None:
                s = jnp.where(allowed, s, -jnp.inf)
            scores.append(s)
            vals.append(vb)
        top = scores[0].max(axis=-1, keepdims=True)
        for s in scores[1:]:
            top = jnp.maximum(top, s.max(axis=-1, keepdims=True))
        expo = [jnp.exp(s - top) for s in scores]
        total = expo[0].sum(axis=-1, keepdims=True)
        for x in expo[1:]:
            total = total + x.sum(axis=-1, keepdims=True)
        inverse = 1.0 / total
        out = None
        for x, vb in zip(expo, vals):
            weight = (x * inverse).astype(BF)
            if vb is None:
                probs_ref[:, head * step : (head + 1) * step] = weight
                continue
            part = nn(weight, vb)
            out = part if out is None else out + part
        out_ref[place * step : (place + 1) * step, q.cols] = out


def attend(first, queries, keys, values, halo, blocks, size):
    heads = queries.shape[1] // size
    args = (first, queries, keys, values, *halo)
    out = spec((len(blocks) * 256, queries.shape[1]), F32)
    return call(
        functools.partial(attend_body, heads, size, blocks),
        (out, spec((256, heads * 256), BF)) if halo else out,
        args,
        [SM] + [VM] * (len(args) - 1),
        flops=1 << 30,
    )


def mix_body(features, heads, r_ref, z_ref, low_ref, high_ref, probs_ref, late_ref, out, buf, sems):
    tokens, width = buf.shape
    size = width // heads
    step = 128
    half = low_ref.shape[0]
    inverse = 1.0 / jnp.sqrt(r_ref[...] / features + EPS)
    copies = []
    for index in reversed(range(tokens // step)):
        start = index * step
        column = jnp.broadcast_to(inverse[:, start : start + step], (128, step)).T[:, 0:1]
        attn = low_ref[start : start + step] if start < half else high_ref[start - half : start - half + step]
        if start < 256:
            keys = late_ref.shape[0]
            parts = [
                nn(probs_ref[start : start + step, h * keys : (h + 1) * keys], late_ref[:, h * size : (h + 1) * size])
                for h in range(heads)
            ]
            attn = attn + jnp.concatenate(parts, axis=1)
        buf[start : start + step] = attn + z_ref[start : start + step] * column
        made = pltpu.make_async_copy(buf.at[start : start + step], out.at[start : start + step], sems.at[index])
        made.start()
        copies.append(made)
    for made in copies:
        made.wait()


def mix(total, z, low, high, probs, late, features, heads):
    scratch = (pltpu.VMEM(z.shape, F32), pltpu.SemaphoreType.DMA((z.shape[0] // 128,)))
    args = (total, z, low, high, probs, late)
    body = functools.partial(mix_body, features, heads)
    return call(body, spec(z.shape, F32), args, away=True, scratch=scratch)


def swap(x, axis, mask):
    return lax.ppermute(x, axis, [(i, i ^ mask) for i in range(lax.axis_size(axis))])


def after(x, *others):
    return lax.optimization_barrier((x, *others))[0]


def plan(place, devices, kind):
    bits = [(place >> n) & 1 for n in range(3)]
    rest = [1 << n for n in range(3, devices.bit_length() - 1)]
    if kind == 0:
        return bits[0] + 2 * (bits[1] ^ bits[2]), (1, 2, 3), ORDERS[0], [6, *rest]
    return bits[1] + 2 * bits[2], (2, 4, 6), ORDERS[1], [1, *rest]


def per_device(queries, keys, values, rates, head_scale, w_one, w_three, w_two):
    tokens, _ = queries.shape
    heads, size = w_one.shape[0], w_one.shape[1]
    rows = 3 * size // 4
    devices = lax.axis_size("seq")
    place = lax.axis_index("seq").astype(jnp.int32)
    first = (place == 0).astype(jnp.int32).reshape(1)
    blocks = tuple(range(tokens // 256))
    half = len(blocks) // 2
    wire = spec((heads, rows + PAD, size), WIRE)
    line = [(i, i + 1) for i in range(devices - 1)]
    ring = [*line, (devices - 1, 0)]
    quarter, masks, order, shared = plan(place, devices, KIND)
    quarter = quarter.reshape(1)

    def spread(parts):
        out = {}
        for j in order:
            out[j] = swap(parts[j - 1], "seq", masks[j - 1])
        return out[1], out[2], out[3]

    halo = [lax.ppermute(tail(keys), "seq", ring)]
    out = grads(quarter, queries, keys, values, rates.T, w_one, w_three, w_two)
    own, p1, p2, p3, mine_w, q, k, v, end, rest, part = out
    got = spread((p1, p2, p3))
    halo.append(lax.ppermute(part, "seq", ring))
    high = attend(first, q, k, v, (), blocks[half:], size)
    mine = call(gather_body, wire, (after(own, high), *got))
    for mask in shared[:-1]:
        mine = call(cross_body, wire, (mine, swap(mine, "seq", mask)))
    other = near(swap(mine, "seq", shared[-1]))[0]
    halo.append(lax.ppermute(after(end, mine), "seq", line))
    scratch = (pltpu.VMEM((heads, rows, size), F32), pltpu.SemaphoreType.DMA)
    new = call(renorm_body, wire, (mine_w, mine, other), [FAR, VM, VM], scratch=scratch)
    pieces = (new, *spread((new, new, new)))
    late = lax.ppermute(after(rest, *pieces), "seq", ring)
    low, probs = attend(first, q, after(k, new), v, halo, blocks[:half], size)
    pieces = (after(new, low), *pieces[1:])
    zed, total, new_t = apply(quarter, q, head_scale, pieces)
    mask = 1
    while mask < lax.axis_size("head"):
        total = total + swap(total, "head", mask)
        mask *= 2
    new_one, new_three, new_two = weights(new_t)
    features = heads * lax.axis_size("head") * size
    mixed = mix(total, zed, low, high, probs, late, features, heads)
    return (mixed, new_one, new_three, new_two)


def solution(mesh):
    placed = (
        P("seq", "head"),
        P("seq", "head"),
        P("seq", "head"),
        P("seq", "head"),
        P("head"),
        P("head", None, None),
        P("head", None, None),
        P("head", None, None),
    )
    return jax.shard_map(
        per_device,
        mesh=mesh,
        in_specs=placed,
        out_specs=(
            P("seq", "head"),
            P("head", None, None),
            P("head", None, None),
            P("head", None, None),
        ),
        check_vma=False,
    )
```

```python
import functools

import jax
import jax.numpy as jnp
from jax import lax
from jax.experimental import pallas as pl
from jax.experimental.pallas import tpu as pltpu
from jax.sharding import PartitionSpec as P


WINDOW_SPAN = 512
EPS = 1e-06
PAD = 8
CUT = 128
KIND = 0
ORDERS = ((1, 2, 3), (2, 1, 3))
WIRE = jnp.bfloat16
REACH = 120.0
BF = jnp.bfloat16
F32 = jnp.float32


def params(mib=24):
    return pltpu.CompilerParams(vmem_limit_bytes=mib * 1024 * 1024)


VM = pl.BlockSpec(memory_space=pltpu.VMEM)
SM = pl.BlockSpec(memory_space=pltpu.SMEM)
FAR = pl.BlockSpec(memory_space=pltpu.HBM)


def call(body, outs, args, specs=None, away=False, scratch=(), flops=0):
    many = isinstance(outs, (tuple, list))
    listed = list(outs) if many else [outs]
    away = list(away) if isinstance(away, tuple) else [away] * len(listed)
    made = [pltpu.HBM(o.shape, o.dtype) if a else pltpu.VMEM(o.shape, o.dtype) for o, a in zip(listed, away)]
    places = [FAR if a else VM for a in away]
    return pl.pallas_call(
        body,
        out_shape=tuple(made) if many else made[0],
        in_specs=specs or [VM] * len(args),
        out_specs=tuple(places) if many else places[0],
        scratch_shapes=list(scratch),
        compiler_params=params(),
        cost_estimate=pl.CostEstimate(flops=flops or 1 << 24, bytes_accessed=1 << 21, transcendentals=0),
    )(*args)


def spec(shape, dtype):
    return jax.ShapeDtypeStruct(shape, dtype)


def nn(a, b):
    return lax.dot_general(a, b, (((1,), (0,)), ((), ())), preferred_element_type=F32)


def nt(a, b):
    return lax.dot_general(a, b, (((1,), (1,)), ((), ())), preferred_element_type=F32)


def split(x):
    high = x.astype(BF)
    return high, (x - high.astype(F32)).astype(BF)


def encode(x, ref):
    rows, size = x.shape
    top = jnp.max(jnp.abs(x), axis=1, keepdims=True)
    scale = (jnp.maximum(top, 1e-30) * 1.008).astype(WIRE).astype(F32)
    code = jnp.exp2(jnp.abs(x) * (2.0 * REACH / scale) - REACH)
    ref[0:rows] = jnp.where(x < 0, -code, code).astype(WIRE)
    column = jnp.concatenate([scale, jnp.zeros((size - rows, 1), F32)], axis=0)
    ref[rows : rows + PAD] = jnp.broadcast_to(column, (size, 128)).T[0:PAD].astype(WIRE)


def decode(ref):
    rows = ref.shape[0] - PAD
    scale = ref[rows : rows + PAD].astype(F32).T[0:rows, 0:1]
    code = ref[0:rows].astype(F32)
    size = (jnp.log2(jnp.abs(code)) + REACH) * (scale * (0.5 / REACH))
    return jnp.where(code < 0, -size, size)


def grads_body(quarter, q_far, k_far, v_far, r_far, w1_far, w3_far, w2_far, *refs):
    own_far, *wires, mine_far, q_ref, k_ref, v_ref, low_far, high_far, mid_far = refs[:-9]
    acc, part, sent, wire, r_ref, w1_ref, w3_ref, w2_ref, sems = refs[-9:]
    heads, size = w1_ref.shape[0], w1_ref.shape[1]
    tokens = k_ref.shape[0]
    step = min(256, tokens)
    count = tokens // step
    used = []

    def copy(source, target):
        made = pltpu.make_async_copy(source, target, sems.at[len(used)])
        made.start()
        used.append(made)
        return made

    def block(ref, index):
        return ref.at[index * step : (index + 1) * step]

    def fetch(index):
        return copy(block(k_far, index), block(k_ref, index)), copy(block(v_far, index), block(v_ref, index))

    def weights_of(head):
        return [copy(a.at[head], b.at[head]) for a, b in ((w1_far, w1_ref), (w3_far, w3_ref), (w2_far, w2_ref))]

    first = [weights_of(0)]
    coming = [fetch(0)]
    rates = copy(r_far, r_ref)
    coming += [fetch(later) for later in range(1, count)]
    late = []
    rows = 3 * size // 4
    q = quarter[0]
    own_rows = pl.ds(pl.multiple_of(q * rows, 8), rows)
    edge = tokens - WINDOW_SPAN
    for head in range(heads):
        first[head][0].wait()
        w1t = w1_ref[head].T
        w1h, w1l = split(w1t)
        first[head][1].wait()
        w3t = w3_ref[head].T
        w3h, w3l = split(w3t)
        first[head][2].wait()
        w2 = w2_ref[head]
        w2h, w2l = split(w2)
        acc[0:size] = w1t
        acc[size : 2 * size] = w3t
        acc[2 * size : 3 * size] = w2.T
        part[head] = acc[own_rows]
        late.append(copy(part.at[head], mine_far.at[head]))
        g1 = g3 = g2 = None
        cols = slice(head * size, (head + 1) * size)
        for index in range(count):
            if head == 0:
                for made in coming[index]:
                    made.wait()
                if index == 0:
                    rates.wait()
                    first += [weights_of(later) for later in range(1, heads)]
                    late.append(copy(q_far, q_ref))
            start = index * step
            kb = k_ref[start : start + step, cols]
            vb = v_ref[start : start + step, cols]
            rate = r_ref[head : head + 1, start : start + step]
            kk = jnp.concatenate([kb, kb], axis=1)
            h1 = nt(jnp.concatenate([w1h, w1l], axis=1), kk)
            h3 = nt(jnp.concatenate([w3h, w3l], axis=1), kk)
            da = nt(jnp.concatenate([w2h, w2l], axis=1), jnp.concatenate([vb, vb], axis=1)) * rate
            sg = 1.0 / (1.0 + jnp.exp(-h1))
            sil = h1 * sg
            act = sil * h3 * rate
            d3 = da * sil
            d1 = da * h3 * (sg * (1.0 + h1 * (1.0 - sg)))
            ah, al = split(act)
            d1h, d1l = split(d1)
            d3h, d3l = split(d3)
            kk = jnp.concatenate([kb, kb], axis=0)
            t1 = nn(jnp.concatenate([d1h, d1l], axis=1), kk)
            t3 = nn(jnp.concatenate([d3h, d3l], axis=1), kk)
            t2 = nn(jnp.concatenate([ah, al], axis=1), jnp.concatenate([vb, vb], axis=0))
            g1 = t1 if g1 is None else g1 + t1
            g3 = t3 if g3 is None else g3 + t3
            g2 = t2 if g2 is None else g2 + t2
        if head == 0:
            middle = edge + WINDOW_SPAN // 2
            late.append(copy(k_ref.at[edge : edge + CUT], mid_far))
            late.append(copy(v_ref.at[middle:], low_far))
            late.append(copy(v_ref.at[edge:middle], high_far))
        acc[0:size] = g1
        acc[size : 2 * size] = g3
        acc[2 * size : 3 * size] = g2.T
        for j, far_ref in enumerate(wires, 1):
            encode(acc[pl.ds(pl.multiple_of((q ^ j) * rows, 8), rows)], wire.at[head, j - 1])
            late.append(copy(wire.at[head, j - 1], far_ref.at[head]))
        sent[head] = acc[own_rows]
        late.append(copy(sent.at[head], own_far.at[head]))
    for made in late:
        made.wait()


def far(*args):
    return [pltpu.with_memory_space_constraint(a, pltpu.HBM) for a in args]


def near(*args):
    return [pltpu.with_memory_space_constraint(a, pltpu.VMEM) for a in args]


def grads(quarter, queries, keys, values, rates_t, w1, w3, w2):
    heads, size = w1.shape[0], w1.shape[1]
    rows = 3 * size // 4
    whole = pltpu.VMEM(w1.shape, F32)
    step = min(256, keys.shape[0])
    copies = 1 + 3 * heads + 2 * (keys.shape[0] // step) + 1 + 5 * heads + 3
    scratch = (
        pltpu.VMEM((3 * size, size), F32),
        pltpu.VMEM((heads, rows, size), F32),
        pltpu.VMEM((heads, rows, size), F32),
        pltpu.VMEM((heads, 3, rows + PAD, size), WIRE),
        pltpu.VMEM(rates_t.shape, F32),
        whole,
        whole,
        whole,
        pltpu.SemaphoreType.DMA((copies,)),
    )
    wire = spec((heads, rows + PAD, size), WIRE)
    part = spec((heads, rows, size), F32)
    inputs = [spec(a.shape, a.dtype) for a in (queries, keys, values)]
    half = (WINDOW_SPAN // 2, keys.shape[1])
    outs = (part, wire, wire, wire, part, *inputs, spec(half, keys.dtype), spec(half, keys.dtype), spec((CUT, keys.shape[1]), keys.dtype))
    away = (True, True, True, True, True, False, False, False, True, True, True)
    args = (quarter, *far(queries, keys, values, rates_t, w1, w3, w2))
    return call(grads_body, outs, args, [SM] + [FAR] * 7, away, scratch, 1 << 31)


def tail_body(k_far, out_ref, sem):
    made = pltpu.make_async_copy(k_far.at[k_far.shape[0] - out_ref.shape[0] :], out_ref, sem)
    made.start()
    made.wait()


def tail(keys):
    out = spec((WINDOW_SPAN - CUT, keys.shape[1]), keys.dtype)
    return call(tail_body, out, far(keys), [FAR], False, (pltpu.SemaphoreType.DMA,))


class Rows:
    def __init__(self, ref, head, size, step):
        self.ref, self.step, self.count = ref, step, ref.shape[0] // step
        self.cols = slice(head * size, (head + 1) * size)

    def at(self, index):
        return self.ref.at[index * self.step : (index + 1) * self.step, self.cols]

    def __call__(self, index):
        return self.ref[index * self.step : (index + 1) * self.step, self.cols]


def heads_of(ref):
    return range(ref.shape[0])


def gather_body(own_ref, r1_ref, r2_ref, r3_ref, out_ref):
    for h in heads_of(out_ref):
        pair = decode(r2_ref.at[h]) + decode(r3_ref.at[h])
        encode(own_ref[h] + decode(r1_ref.at[h]) + pair, out_ref.at[h])


def cross_body(mine_ref, other_ref, out_ref):
    for h in heads_of(out_ref):
        encode(decode(mine_ref.at[h]) + decode(other_ref.at[h]), out_ref.at[h])


def renorm_body(w_far, mine_ref, other_ref, out_ref, w_ref, sem):
    fetch = pltpu.make_async_copy(w_far, w_ref, sem)
    fetch.start()
    sums = [decode(mine_ref.at[h]) + decode(other_ref.at[h]) for h in heads_of(out_ref)]
    fetch.wait()
    for h, total in enumerate(sums):
        w = w_ref[h]
        upd = w + total
        old = jnp.sqrt(jnp.sum(w * w, axis=1, keepdims=True) + EPS)
        cur = jnp.sqrt(jnp.sum(upd * upd, axis=1, keepdims=True) + EPS)
        encode(upd * (old / cur), out_ref.at[h])


def apply_body(quarter, s_ref, q_ref, own_ref, r1_ref, r2_ref, r3_ref, z_ref, sq_ref, n_ref):
    heads, rows, size = own_ref.shape
    rows -= PAD
    tokens = q_ref.shape[0]
    q = quarter[0]
    block = min(1024, tokens)
    for head in range(heads):
        for j, ref in enumerate((own_ref, r1_ref, r2_ref, r3_ref)):
            n_ref[head, pl.ds(pl.multiple_of((q ^ j) * rows, 8), rows)] = decode(ref.at[head])
        n1h, n1l = split(n_ref[head, 0:size])
        n3h, n3l = split(n_ref[head, size : 2 * size])
        n2h, n2l = split(n_ref[head, 2 * size : 3 * size])
        scale = s_ref[head]
        for start in range(0, tokens, block):
            qb = q_ref[start : start + block, head * size : (head + 1) * size]
            qq = jnp.concatenate([qb, qb], axis=1)
            p1 = nt(qq, jnp.concatenate([n1h, n1l], axis=1))
            p3 = nt(qq, jnp.concatenate([n3h, n3l], axis=1))
            hh, hl = split(p1 * (1.0 / (1.0 + jnp.exp(-p1))) * p3)
            zed = nt(jnp.concatenate([hh, hl, hh], axis=1), jnp.concatenate([n2h, n2h, n2l], axis=1)) * scale
            z_ref[start : start + block, head * size : (head + 1) * size] = zed
            zz = zed * zed
            half = zz[:, 0:128]
            for lane in range(128, size, 128):
                half = half + zz[:, lane : lane + 128]
            found = jnp.sum(half.T, axis=0, keepdims=True)
            if head == 0:
                sq_ref[:, start : start + block] = found
            else:
                sq_ref[:, start : start + block] += found


def apply(quarter, queries, scale, pieces):
    heads, _, size = pieces[0].shape
    tokens = queries.shape[0]
    outs = (spec((tokens, heads * size), F32), spec((1, tokens), F32), spec((heads, 3 * size, size), F32))
    args = (quarter, scale, queries, *pieces)
    return call(apply_body, outs, args, [SM, SM] + [VM] * 5, flops=1 << 31)


def weights_body(n_ref, o1, o3, o2, buf, sems):
    size = o1.shape[1]
    copies = []
    for head in heads_of(n_ref):
        for place, out in enumerate((o1, o3, o2)):
            index = 3 * head + place
            buf[index] = n_ref[head, place * size : (place + 1) * size].T
            made = pltpu.make_async_copy(buf.at[index], out.at[head], sems.at[index])
            made.start()
            copies.append(made)
    for made in copies:
        made.wait()


def weights(new):
    heads, _, size = new.shape
    square = spec((heads, size, size), F32)
    scratch = (pltpu.VMEM((3 * heads, size, size), F32), pltpu.SemaphoreType.DMA((3 * heads,)))
    return call(weights_body, (square,) * 3, (new,), away=True, scratch=scratch)


def attend_body(heads, size, blocks, *refs):
    for head in range(heads):
        attend_head(head, size, blocks, *refs)


def attend_head(head, size, blocks, first_ref, q_ref, k_ref, v_ref, *refs):
    early, part, mid = refs[:3] if len(refs) > 1 else (None, None, None)
    out_ref, probs_ref = (refs[3], refs[4]) if len(refs) > 1 else (refs[0], None)
    step = 256
    span = WINDOW_SPAN // step
    scale = size ** (-0.5)
    q, k, v = (Rows(ref, head, size, step) for ref in (q_ref, k_ref, v_ref))
    rows = lax.broadcasted_iota(jnp.int32, (step, step), 0)
    cols = lax.broadcasted_iota(jnp.int32, (step, step), 1)
    for place, block in enumerate(blocks):
        qb = q(block)
        scores, vals = [], []
        for back in range(span, -1, -1):
            source = block - back
            if source < 0:
                at = (source + span) * step
                if at == 0:
                    kb, vb = jnp.concatenate([part[:, q.cols], early[0 : step - CUT, q.cols]], axis=0), None
                else:
                    kb, vb = early[at - CUT : at - CUT + step, q.cols], mid[:, q.cols]
            else:
                kb, vb = k(source), v(source)
            s = nt(qb, kb) * scale
            allowed = None
            if back == 0:
                allowed = cols <= rows
            if back == span:
                allowed = cols > rows
            if source < 0:
                here = first_ref[0] == 0
                allowed = here if allowed is None else allowed & here
            if allowed is not None:
                s = jnp.where(allowed, s, -jnp.inf)
            scores.append(s)
            vals.append(vb)
        top = scores[0].max(axis=-1, keepdims=True)
        for s in scores[1:]:
            top = jnp.maximum(top, s.max(axis=-1, keepdims=True))
        expo = [jnp.exp(s - top) for s in scores]
        total = expo[0].sum(axis=-1, keepdims=True)
        for x in expo[1:]:
            total = total + x.sum(axis=-1, keepdims=True)
        inverse = 1.0 / total
        out = None
        for x, vb in zip(expo, vals):
            weight = (x * inverse).astype(BF)
            if vb is None:
                probs_ref[:, head * step : (head + 1) * step] = weight
                continue
            part = nn(weight, vb)
            out = part if out is None else out + part
        out_ref[place * step : (place + 1) * step, q.cols] = out


def attend(first, queries, keys, values, halo, blocks, size):
    heads = queries.shape[1] // size
    args = (first, queries, keys, values, *halo)
    out = spec((len(blocks) * 256, queries.shape[1]), F32)
    return call(
        functools.partial(attend_body, heads, size, blocks),
        (out, spec((256, heads * 256), BF)) if halo else out,
        args,
        [SM] + [VM] * (len(args) - 1),
        flops=1 << 30,
    )


def mix_body(features, heads, r_ref, z_ref, low_ref, high_ref, probs_ref, late_ref, out, buf, sems):
    tokens, width = buf.shape
    size = width // heads
    step = 128
    half = low_ref.shape[0]
    inverse = 1.0 / jnp.sqrt(r_ref[...] / features + EPS)
    copies = []
    for index in reversed(range(tokens // step)):
        start = index * step
        column = jnp.broadcast_to(inverse[:, start : start + step], (128, step)).T[:, 0:1]
        attn = low_ref[start : start + step] if start < half else high_ref[start - half : start - half + step]
        if start < 256:
            keys = late_ref.shape[0]
            parts = [
                nn(probs_ref[start : start + step, h * keys : (h + 1) * keys], late_ref[:, h * size : (h + 1) * size])
                for h in range(heads)
            ]
            attn = attn + jnp.concatenate(parts, axis=1)
        buf[start : start + step] = attn + z_ref[start : start + step] * column
        made = pltpu.make_async_copy(buf.at[start : start + step], out.at[start : start + step], sems.at[index])
        made.start()
        copies.append(made)
    for made in copies:
        made.wait()


def mix(total, z, low, high, probs, late, features, heads):
    scratch = (pltpu.VMEM(z.shape, F32), pltpu.SemaphoreType.DMA((z.shape[0] // 128,)))
    args = (total, z, low, high, probs, late)
    body = functools.partial(mix_body, features, heads)
    return call(body, spec(z.shape, F32), args, away=True, scratch=scratch)


def swap(x, axis, mask):
    return lax.ppermute(x, axis, [(i, i ^ mask) for i in range(lax.axis_size(axis))])


def after(x, *others):
    return lax.optimization_barrier((x, *others))[0]


def plan(place, devices, kind):
    bits = [(place >> n) & 1 for n in range(3)]
    rest = [1 << n for n in range(3, devices.bit_length() - 1)]
    if kind == 0:
        return bits[0] + 2 * (bits[1] ^ bits[2]), (1, 2, 3), ORDERS[0], [6, *rest]
    return bits[1] + 2 * bits[2], (2, 4, 6), ORDERS[1], [1, *rest]


def per_device(queries, keys, values, rates, head_scale, w_one, w_three, w_two):
    tokens, _ = queries.shape
    heads, size = w_one.shape[0], w_one.shape[1]
    rows = 3 * size // 4
    devices = lax.axis_size("seq")
    place = lax.axis_index("seq").astype(jnp.int32)
    first = (place == 0).astype(jnp.int32).reshape(1)
    blocks = tuple(range(tokens // 256))
    half = len(blocks) // 2
    wire = spec((heads, rows + PAD, size), WIRE)
    line = [(i, i + 1) for i in range(devices - 1)]
    ring = [*line, (devices - 1, 0)]
    quarter, masks, order, shared = plan(place, devices, KIND)
    quarter = quarter.reshape(1)

    def spread(parts):
        out = {}
        for j in order:
            out[j] = swap(parts[j - 1], "seq", masks[j - 1])
        return out[1], out[2], out[3]

    halo = [lax.ppermute(tail(keys), "seq", ring)]
    out = grads(quarter, queries, keys, values, rates.T, w_one, w_three, w_two)
    own, p1, p2, p3, mine_w, q, k, v, end, rest, part = out
    got = spread((p1, p2, p3))
    halo.append(lax.ppermute(part, "seq", ring))
    high = attend(first, q, k, v, (), blocks[half:], size)
    mine = call(gather_body, wire, (after(own, high), *got))
    for mask in shared[:-1]:
        mine = call(cross_body, wire, (mine, swap(mine, "seq", mask)))
    other = near(swap(mine, "seq", shared[-1]))[0]
    halo.append(lax.ppermute(after(end, mine), "seq", line))
    scratch = (pltpu.VMEM((heads, rows, size), F32), pltpu.SemaphoreType.DMA)
    new = call(renorm_body, wire, (mine_w, mine, other), [FAR, VM, VM], scratch=scratch)
    pieces = (new, *spread((new, new, new)))
    late = lax.ppermute(after(rest, pieces[1]), "seq", ring)
    low, probs = attend(first, q, after(k, new), v, halo, blocks[:half], size)
    pieces = (after(new, low), *pieces[1:])
    zed, total, new_t = apply(quarter, q, head_scale, pieces)
    mask, reach = 1, lax.axis_size("head")
    while mask < reach:
        masks = (3 * mask, 2 * mask, mask) if 4 * mask <= reach else (mask,)
        parts = []
        for m in masks:
            parts.append(swap(total, "head", m))
        total = sum(parts, total)
        mask *= len(masks) + 1
    new_one, new_three, new_two = weights(new_t)
    features = heads * lax.axis_size("head") * size
    mixed = mix(total, zed, low, high, probs, late, features, heads)
    return (mixed, new_one, new_three, new_two)


def solution(mesh):
    placed = (
        P("seq", "head"),
        P("seq", "head"),
        P("seq", "head"),
        P("seq", "head"),
        P("head"),
        P("head", None, None),
        P("head", None, None),
        P("head", None, None),
    )
    return jax.shard_map(
        per_device,
        mesh=mesh,
        in_specs=placed,
        out_specs=(
            P("seq", "head"),
            P("head", None, None),
            P("head", None, None),
            P("head", None, None),
        ),
        check_vma=False,
    )
```

```python
import functools

import jax
import jax.numpy as jnp
from jax import lax
from jax.experimental import pallas as pl
from jax.experimental.pallas import tpu as pltpu
from jax.sharding import PartitionSpec as P


WINDOW_SPAN = 512
EPS = 1e-06
PAD = 8
CUT = 192
KIND = 0
ORDERS = ((1, 2, 3), (2, 1, 3))
WIRE = jnp.bfloat16
REACH = 120.0
BF = jnp.bfloat16
F32 = jnp.float32


def params(mib=24):
    return pltpu.CompilerParams(vmem_limit_bytes=mib * 1024 * 1024)


VM = pl.BlockSpec(memory_space=pltpu.VMEM)
SM = pl.BlockSpec(memory_space=pltpu.SMEM)
FAR = pl.BlockSpec(memory_space=pltpu.HBM)


def call(body, outs, args, specs=None, away=False, scratch=(), flops=0):
    many = isinstance(outs, (tuple, list))
    listed = list(outs) if many else [outs]
    away = list(away) if isinstance(away, tuple) else [away] * len(listed)
    made = [pltpu.HBM(o.shape, o.dtype) if a else pltpu.VMEM(o.shape, o.dtype) for o, a in zip(listed, away)]
    places = [FAR if a else VM for a in away]
    return pl.pallas_call(
        body,
        out_shape=tuple(made) if many else made[0],
        in_specs=specs or [VM] * len(args),
        out_specs=tuple(places) if many else places[0],
        scratch_shapes=list(scratch),
        compiler_params=params(),
        cost_estimate=pl.CostEstimate(flops=flops or 1 << 24, bytes_accessed=1 << 21, transcendentals=0),
    )(*args)


def spec(shape, dtype):
    return jax.ShapeDtypeStruct(shape, dtype)


def nn(a, b):
    return lax.dot_general(a, b, (((1,), (0,)), ((), ())), preferred_element_type=F32)


def nt(a, b):
    return lax.dot_general(a, b, (((1,), (1,)), ((), ())), preferred_element_type=F32)


def split(x):
    high = x.astype(BF)
    return high, (x - high.astype(F32)).astype(BF)


def encode(x, ref):
    rows, size = x.shape
    top = jnp.max(jnp.abs(x), axis=1, keepdims=True)
    scale = (jnp.maximum(top, 1e-30) * 1.008).astype(WIRE).astype(F32)
    code = jnp.exp2(jnp.abs(x) * (2.0 * REACH / scale) - REACH)
    ref[0:rows] = jnp.where(x < 0, -code, code).astype(WIRE)
    column = jnp.concatenate([scale, jnp.zeros((size - rows, 1), F32)], axis=0)
    ref[rows : rows + PAD] = jnp.broadcast_to(column, (size, 128)).T[0:PAD].astype(WIRE)


def decode(ref):
    rows = ref.shape[0] - PAD
    scale = ref[rows : rows + PAD].astype(F32).T[0:rows, 0:1]
    code = ref[0:rows].astype(F32)
    size = (jnp.log2(jnp.abs(code)) + REACH) * (scale * (0.5 / REACH))
    return jnp.where(code < 0, -size, size)


def grads_body(quarter, q_far, k_far, v_far, r_far, w1_far, w3_far, w2_far, *refs):
    own_far, *wires, mine_far, q_ref, k_ref, v_ref, low_far, high_far, mid_far = refs[:-9]
    acc, part, sent, wire, r_ref, w1_ref, w3_ref, w2_ref, sems = refs[-9:]
    heads, size = w1_ref.shape[0], w1_ref.shape[1]
    tokens = k_ref.shape[0]
    step = min(512, tokens)
    count = tokens // step
    used = []

    def copy(source, target):
        made = pltpu.make_async_copy(source, target, sems.at[len(used)])
        made.start()
        used.append(made)
        return made

    def block(ref, index):
        return ref.at[index * step : (index + 1) * step]

    def fetch(index):
        return copy(block(k_far, index), block(k_ref, index)), copy(block(v_far, index), block(v_ref, index))

    def weights_of(head):
        return [copy(a.at[head], b.at[head]) for a, b in ((w1_far, w1_ref), (w3_far, w3_ref), (w2_far, w2_ref))]

    first = [weights_of(0)]
    coming = [fetch(0)]
    rates = copy(r_far, r_ref)
    coming += [fetch(later) for later in range(1, count)]
    late = []
    rows = 3 * size // 4
    q = quarter[0]
    own_rows = pl.ds(pl.multiple_of(q * rows, 8), rows)
    edge = tokens - WINDOW_SPAN
    for head in range(heads):
        first[head][0].wait()
        w1t = w1_ref[head].T
        w1h, w1l = split(w1t)
        first[head][1].wait()
        w3t = w3_ref[head].T
        w3h, w3l = split(w3t)
        first[head][2].wait()
        w2 = w2_ref[head]
        w2h, w2l = split(w2)
        acc[0:size] = w1t
        acc[size : 2 * size] = w3t
        acc[2 * size : 3 * size] = w2.T
        part[head] = acc[own_rows]
        late.append(copy(part.at[head], mine_far.at[head]))
        g1 = g3 = g2 = None
        cols = slice(head * size, (head + 1) * size)
        for index in range(count):
            if head == 0:
                for made in coming[index]:
                    made.wait()
                if index == 0:
                    rates.wait()
                    first += [weights_of(later) for later in range(1, heads)]
                    late.append(copy(q_far, q_ref))
            start = index * step
            kb = k_ref[start : start + step, cols]
            vb = v_ref[start : start + step, cols]
            rate = r_ref[head : head + 1, start : start + step]
            kk = jnp.concatenate([kb, kb], axis=1)
            h1 = nt(jnp.concatenate([w1h, w1l], axis=1), kk)
            h3 = nt(jnp.concatenate([w3h, w3l], axis=1), kk)
            da = nt(jnp.concatenate([w2h, w2l], axis=1), jnp.concatenate([vb, vb], axis=1)) * rate
            sg = 1.0 / (1.0 + jnp.exp(-h1))
            sil = h1 * sg
            act = sil * h3 * rate
            d3 = da * sil
            d1 = da * h3 * (sg * (1.0 + h1 * (1.0 - sg)))
            ah, al = split(act)
            d1h, d1l = split(d1)
            d3h, d3l = split(d3)
            kk = jnp.concatenate([kb, kb], axis=0)
            t1 = nn(jnp.concatenate([d1h, d1l], axis=1), kk)
            t3 = nn(jnp.concatenate([d3h, d3l], axis=1), kk)
            t2 = nn(jnp.concatenate([ah, al], axis=1), jnp.concatenate([vb, vb], axis=0))
            g1 = t1 if g1 is None else g1 + t1
            g3 = t3 if g3 is None else g3 + t3
            g2 = t2 if g2 is None else g2 + t2
        if head == 0:
            middle = edge + WINDOW_SPAN // 2
            late.append(copy(k_ref.at[edge : edge + CUT], mid_far))
            late.append(copy(v_ref.at[middle:], low_far))
            late.append(copy(v_ref.at[edge:middle], high_far))
        acc[0:size] = g1
        acc[size : 2 * size] = g3
        acc[2 * size : 3 * size] = g2.T
        for j, far_ref in enumerate(wires, 1):
            encode(acc[pl.ds(pl.multiple_of((q ^ j) * rows, 8), rows)], wire.at[head, j - 1])
            late.append(copy(wire.at[head, j - 1], far_ref.at[head]))
        sent[head] = acc[own_rows]
        late.append(copy(sent.at[head], own_far.at[head]))
    for made in late:
        made.wait()


def far(*args):
    return [pltpu.with_memory_space_constraint(a, pltpu.HBM) for a in args]


def near(*args):
    return [pltpu.with_memory_space_constraint(a, pltpu.VMEM) for a in args]


def grads(quarter, queries, keys, values, rates_t, w1, w3, w2):
    heads, size = w1.shape[0], w1.shape[1]
    rows = 3 * size // 4
    whole = pltpu.VMEM(w1.shape, F32)
    step = min(512, keys.shape[0])
    copies = 1 + 3 * heads + 2 * (keys.shape[0] // step) + 1 + 5 * heads + 3
    scratch = (
        pltpu.VMEM((3 * size, size), F32),
        pltpu.VMEM((heads, rows, size), F32),
        pltpu.VMEM((heads, rows, size), F32),
        pltpu.VMEM((heads, 3, rows + PAD, size), WIRE),
        pltpu.VMEM(rates_t.shape, F32),
        whole,
        whole,
        whole,
        pltpu.SemaphoreType.DMA((copies,)),
    )
    wire = spec((heads, rows + PAD, size), WIRE)
    part = spec((heads, rows, size), F32)
    inputs = [spec(a.shape, a.dtype) for a in (queries, keys, values)]
    half = (WINDOW_SPAN // 2, keys.shape[1])
    outs = (part, wire, wire, wire, part, *inputs, spec(half, keys.dtype), spec(half, keys.dtype), spec((CUT, keys.shape[1]), keys.dtype))
    away = (True, True, True, True, True, False, False, False, True, True, True)
    args = (quarter, *far(queries, keys, values, rates_t, w1, w3, w2))
    return call(grads_body, outs, args, [SM] + [FAR] * 7, away, scratch, 1 << 31)


def tail_body(k_far, out_ref, sem):
    made = pltpu.make_async_copy(k_far.at[k_far.shape[0] - out_ref.shape[0] :], out_ref, sem)
    made.start()
    made.wait()


def tail(keys):
    out = spec((WINDOW_SPAN - CUT, keys.shape[1]), keys.dtype)
    return call(tail_body, out, far(keys), [FAR], False, (pltpu.SemaphoreType.DMA,))


class Rows:
    def __init__(self, ref, head, size, step):
        self.ref, self.step, self.count = ref, step, ref.shape[0] // step
        self.cols = slice(head * size, (head + 1) * size)

    def at(self, index):
        return self.ref.at[index * self.step : (index + 1) * self.step, self.cols]

    def __call__(self, index):
        return self.ref[index * self.step : (index + 1) * self.step, self.cols]


def heads_of(ref):
    return range(ref.shape[0])


def gather_body(own_ref, r1_ref, r2_ref, r3_ref, out_ref):
    for h in heads_of(out_ref):
        pair = decode(r2_ref.at[h]) + decode(r3_ref.at[h])
        encode(own_ref[h] + decode(r1_ref.at[h]) + pair, out_ref.at[h])


def cross_body(mine_ref, other_ref, out_ref):
    for h in heads_of(out_ref):
        encode(decode(mine_ref.at[h]) + decode(other_ref.at[h]), out_ref.at[h])


def renorm_body(w_far, mine_ref, other_ref, out_ref, w_ref, sem):
    fetch = pltpu.make_async_copy(w_far, w_ref, sem)
    fetch.start()
    sums = [decode(mine_ref.at[h]) + decode(other_ref.at[h]) for h in heads_of(out_ref)]
    fetch.wait()
    for h, total in enumerate(sums):
        w = w_ref[h]
        upd = w + total
        old = jnp.sqrt(jnp.sum(w * w, axis=1, keepdims=True) + EPS)
        cur = jnp.sqrt(jnp.sum(upd * upd, axis=1, keepdims=True) + EPS)
        encode(upd * (old / cur), out_ref.at[h])


def apply_body(quarter, s_ref, q_ref, own_ref, r1_ref, r2_ref, r3_ref, z_ref, sq_ref, n_ref):
    heads, rows, size = own_ref.shape
    rows -= PAD
    tokens = q_ref.shape[0]
    q = quarter[0]
    block = min(1024, tokens)
    for head in range(heads):
        for j, ref in enumerate((own_ref, r1_ref, r2_ref, r3_ref)):
            n_ref[head, pl.ds(pl.multiple_of((q ^ j) * rows, 8), rows)] = decode(ref.at[head])
        n1h, n1l = split(n_ref[head, 0:size])
        n3h, n3l = split(n_ref[head, size : 2 * size])
        n2h, n2l = split(n_ref[head, 2 * size : 3 * size])
        scale = s_ref[head]
        for start in range(0, tokens, block):
            qb = q_ref[start : start + block, head * size : (head + 1) * size]
            qq = jnp.concatenate([qb, qb], axis=1)
            p1 = nt(qq, jnp.concatenate([n1h, n1l], axis=1))
            p3 = nt(qq, jnp.concatenate([n3h, n3l], axis=1))
            hh, hl = split(p1 * (1.0 / (1.0 + jnp.exp(-p1))) * p3)
            zed = nt(jnp.concatenate([hh, hl, hh], axis=1), jnp.concatenate([n2h, n2h, n2l], axis=1)) * scale
            z_ref[start : start + block, head * size : (head + 1) * size] = zed
            zz = zed * zed
            half = zz[:, 0:128]
            for lane in range(128, size, 128):
                half = half + zz[:, lane : lane + 128]
            found = jnp.sum(half.T, axis=0, keepdims=True)
            if head == 0:
                sq_ref[:, start : start + block] = found
            else:
                sq_ref[:, start : start + block] += found


def apply(quarter, queries, scale, pieces):
    heads, _, size = pieces[0].shape
    tokens = queries.shape[0]
    outs = (spec((tokens, heads * size), F32), spec((1, tokens), F32), spec((heads, 3 * size, size), F32))
    args = (quarter, scale, queries, *pieces)
    return call(apply_body, outs, args, [SM, SM] + [VM] * 5, flops=1 << 31)


def weights_body(n_ref, o1, o3, o2, buf, sems):
    size = o1.shape[1]
    copies = []
    for head in heads_of(n_ref):
        for place, out in enumerate((o1, o3, o2)):
            index = 3 * head + place
            buf[index] = n_ref[head, place * size : (place + 1) * size].T
            made = pltpu.make_async_copy(buf.at[index], out.at[head], sems.at[index])
            made.start()
            copies.append(made)
    for made in copies:
        made.wait()


def weights(new):
    heads, _, size = new.shape
    square = spec((heads, size, size), F32)
    scratch = (pltpu.VMEM((3 * heads, size, size), F32), pltpu.SemaphoreType.DMA((3 * heads,)))
    return call(weights_body, (square,) * 3, (new,), away=True, scratch=scratch)


def attend_body(heads, size, blocks, *refs):
    for head in range(heads):
        attend_head(head, size, blocks, *refs)


def attend_head(head, size, blocks, first_ref, q_ref, k_ref, v_ref, *refs):
    early, part, mid = refs[:3] if len(refs) > 1 else (None, None, None)
    out_ref, probs_ref = (refs[3], refs[4]) if len(refs) > 1 else (refs[0], None)
    step = 256
    span = WINDOW_SPAN // step
    scale = size ** (-0.5)
    q, k, v = (Rows(ref, head, size, step) for ref in (q_ref, k_ref, v_ref))
    rows = lax.broadcasted_iota(jnp.int32, (step, step), 0)
    cols = lax.broadcasted_iota(jnp.int32, (step, step), 1)
    for place, block in enumerate(blocks):
        qb = q(block)
        scores, vals = [], []
        for back in range(span, -1, -1):
            source = block - back
            if source < 0:
                at = (source + span) * step
                if at == 0:
                    kb, vb = jnp.concatenate([part[:, q.cols], early[0 : step - CUT, q.cols]], axis=0), None
                else:
                    kb, vb = early[at - CUT : at - CUT + step, q.cols], mid[:, q.cols]
            else:
                kb, vb = k(source), v(source)
            s = nt(qb, kb) * scale
            allowed = None
            if back == 0:
                allowed = cols <= rows
            if back == span:
                allowed = cols > rows
            if source < 0:
                here = first_ref[0] == 0
                allowed = here if allowed is None else allowed & here
            if allowed is not None:
                s = jnp.where(allowed, s, -jnp.inf)
            scores.append(s)
            vals.append(vb)
        top = scores[0].max(axis=-1, keepdims=True)
        for s in scores[1:]:
            top = jnp.maximum(top, s.max(axis=-1, keepdims=True))
        expo = [jnp.exp(s - top) for s in scores]
        total = expo[0].sum(axis=-1, keepdims=True)
        for x in expo[1:]:
            total = total + x.sum(axis=-1, keepdims=True)
        inverse = 1.0 / total
        out = None
        for x, vb in zip(expo, vals):
            weight = (x * inverse).astype(BF)
            if vb is None:
                probs_ref[:, head * step : (head + 1) * step] = weight
                continue
            part = nn(weight, vb)
            out = part if out is None else out + part
        out_ref[place * step : (place + 1) * step, q.cols] = out


def attend(first, queries, keys, values, halo, blocks, size):
    heads = queries.shape[1] // size
    args = (first, queries, keys, values, *halo)
    out = spec((len(blocks) * 256, queries.shape[1]), F32)
    return call(
        functools.partial(attend_body, heads, size, blocks),
        (out, spec((256, heads * 256), BF)) if halo else out,
        args,
        [SM] + [VM] * (len(args) - 1),
        flops=1 << 30,
    )


def mix_body(features, heads, r_ref, z_ref, low_ref, high_ref, probs_ref, late_ref, out, buf, sems):
    tokens, width = buf.shape
    size = width // heads
    step = 128
    half = low_ref.shape[0]
    inverse = 1.0 / jnp.sqrt(r_ref[...] / features + EPS)
    copies = []
    for index in reversed(range(tokens // step)):
        start = index * step
        column = jnp.broadcast_to(inverse[:, start : start + step], (128, step)).T[:, 0:1]
        attn = low_ref[start : start + step] if start < half else high_ref[start - half : start - half + step]
        if start < 256:
            keys = late_ref.shape[0]
            parts = [
                nn(probs_ref[start : start + step, h * keys : (h + 1) * keys], late_ref[:, h * size : (h + 1) * size])
                for h in range(heads)
            ]
            attn = attn + jnp.concatenate(parts, axis=1)
        buf[start : start + step] = attn + z_ref[start : start + step] * column
        made = pltpu.make_async_copy(buf.at[start : start + step], out.at[start : start + step], sems.at[index])
        made.start()
        copies.append(made)
    for made in copies:
        made.wait()


def mix(total, z, low, high, probs, late, features, heads):
    scratch = (pltpu.VMEM(z.shape, F32), pltpu.SemaphoreType.DMA((z.shape[0] // 128,)))
    args = (total, z, low, high, probs, late)
    body = functools.partial(mix_body, features, heads)
    return call(body, spec(z.shape, F32), args, away=True, scratch=scratch)


def swap(x, axis, mask):
    return lax.ppermute(x, axis, [(i, i ^ mask) for i in range(lax.axis_size(axis))])


def after(x, *others):
    return lax.optimization_barrier((x, *others))[0]


def plan(place, devices, kind):
    bits = [(place >> n) & 1 for n in range(3)]
    rest = [1 << n for n in range(3, devices.bit_length() - 1)]
    if kind == 0:
        return bits[0] + 2 * (bits[1] ^ bits[2]), (1, 2, 3), ORDERS[0], [6, *rest]
    return bits[1] + 2 * bits[2], (2, 4, 6), ORDERS[1], [1, *rest]


def per_device(queries, keys, values, rates, head_scale, w_one, w_three, w_two):
    tokens, _ = queries.shape
    heads, size = w_one.shape[0], w_one.shape[1]
    rows = 3 * size // 4
    devices = lax.axis_size("seq")
    place = lax.axis_index("seq").astype(jnp.int32)
    first = (place == 0).astype(jnp.int32).reshape(1)
    blocks = tuple(range(tokens // 256))
    half = len(blocks) // 2
    wire = spec((heads, rows + PAD, size), WIRE)
    line = [(i, i + 1) for i in range(devices - 1)]
    ring = [*line, (devices - 1, 0)]
    quarter, masks, order, shared = plan(place, devices, KIND)
    quarter = quarter.reshape(1)

    def spread(parts):
        out = {}
        for j in order:
            out[j] = swap(parts[j - 1], "seq", masks[j - 1])
        return out[1], out[2], out[3]

    halo = [lax.ppermute(tail(keys), "seq", ring)]
    out = grads(quarter, queries, keys, values, rates.T, w_one, w_three, w_two)
    own, p1, p2, p3, mine_w, q, k, v, end, rest, part = out
    got = spread((p1, p2, p3))
    halo.append(lax.ppermute(part, "seq", line))
    high = attend(first, q, k, v, (), blocks[half:], size)
    mine = call(gather_body, wire, (after(own, high), *got))
    for mask in shared[:-1]:
        mine = call(cross_body, wire, (mine, swap(mine, "seq", mask)))
    other = near(swap(mine, "seq", shared[-1]))[0]
    halo.append(lax.ppermute(after(end, mine), "seq", line))
    scratch = (pltpu.VMEM((heads, rows, size), F32), pltpu.SemaphoreType.DMA)
    new = call(renorm_body, wire, (mine_w, mine, other), [FAR, VM, VM], scratch=scratch)
    pieces = (new, *spread((new, new, new)))
    late = lax.ppermute(after(rest, pieces[1]), "seq", line)
    low, probs = attend(first, q, after(k, new), v, halo, blocks[:half], size)
    pieces = (after(new, low), *pieces[1:])
    zed, total, new_t = apply(quarter, q, head_scale, pieces)
    mask, reach = 1, lax.axis_size("head")
    while mask < reach:
        masks = (3 * mask, 2 * mask, mask) if 4 * mask <= reach else (mask,)
        parts = []
        for m in masks:
            parts.append(swap(total, "head", m))
        total = sum(parts, total)
        mask *= len(masks) + 1
    new_one, new_three, new_two = weights(new_t)
    features = heads * lax.axis_size("head") * size
    mixed = mix(total, zed, low, high, probs, late, features, heads)
    return (mixed, new_one, new_three, new_two)


def solution(mesh):
    placed = (
        P("seq", "head"),
        P("seq", "head"),
        P("seq", "head"),
        P("seq", "head"),
        P("head"),
        P("head", None, None),
        P("head", None, None),
        P("head", None, None),
    )
    return jax.shard_map(
        per_device,
        mesh=mesh,
        in_specs=placed,
        out_specs=(
            P("seq", "head"),
            P("head", None, None),
            P("head", None, None),
            P("head", None, None),
        ),
        check_vma=False,
    )
```
